32 devices in a mesh: seq: 16 (over z, x, core), vocab: 2 (over y).
Axes of the slice: x: 2, y: 2, z: 4, core: 2. Of those that a mesh axis runs over, the one named last changes fastest.
Arguments:
- queries: bfloat16 [3, 4096, 8192], P(None, 'seq', 'vocab'), may hold values from -32 to 32
- draft_kv: bfloat16 [3, 2, 4096, 1024], P(None, None, 'seq', 'vocab'), may hold values from -6 to 6
- doc_ids: int32 [4096], P('seq'), may hold values from 0 to 4, as said below
- logits: bfloat16 [4096, 65536], P('seq', 'vocab'), may hold values from -90 to 360
- targets: int32 [4096], P('seq'), may hold values from 0 to 65535
Outputs:
- attended: bfloat16 [3, 4096, 8192], P(None, 'seq', 'vocab')
- row_peak: float32 [3, 4096, 64], P(None, 'seq', 'vocab')
- token_loss: float32 [4096], P('seq')
The draws below stay inside these ranges and needn't reach their ends.
Inputs may be any that keep to these rules, and one draw needn't show every extreme that they name: `doc_ids`: document ids start at 0, never fall, and rise by one where a new document begins; one document has exactly 3072 tokens, and the other tokens form exactly (4096 - 3072) // 256 documents, each shorter than it.
All inputs are finite; a program needn't handle non-finite values.
Results may differ from the reference program's by a relative error of at most 0.004.
Values may be sent and summed in bfloat16 or wider, within the bound.
No kernel may reach another device: no remote copies, remote signals or barrier semaphores. Data moves between devices by JAX's collectives and lax.ppermute only.
A program may use at most 128 MiB of HBM per device.

```python
import math
import jax
import jax.numpy as jnp
from jax import lax

HEADS = 64
KV = 8
HD = 128
VOCAB = 65536
STEPS = 3
TOK_DEV = 256
TOKENS = 4096
LONG_DOC = 3072


def doc_layout(key):
    base_key = jax.random.fold_in(key, 101)
    cut_key, pick_key = jax.random.split(base_key)
    outside = TOKENS - LONG_DOC
    pieces = outside // TOK_DEV
    shuffled = jax.random.permutation(cut_key, outside - 1) + 1
    cuts = shuffled[:pieces - 1]
    bounds = jnp.sort(jnp.concatenate([jnp.zeros((1,), jnp.int32), cuts.astype(jnp.int32), jnp.full((1,), outside, jnp.int32)]))
    offset = bounds[jax.random.randint(pick_key, (), 0, pieces + 1)]
    position = jnp.arange(TOKENS, dtype=jnp.int32)
    inside = (position >= offset) & (position < offset + LONG_DOC)
    outer = jnp.where(position >= offset + LONG_DOC, position - LONG_DOC, position)
    is_cut = (outer == 0) | jnp.any(outer[:, None] == cuts[None, :].astype(jnp.int32), axis=1)
    begins = jnp.where(inside, position == offset, is_cut)
    running = jnp.cumsum(begins.astype(jnp.int32))
    return (running - 1).astype(jnp.int32)


def draw_doc_ids(key, part):
    return doc_layout(key)


def draw_draft_kv(key, part):
    draw_key = jax.random.fold_in(key, 303)
    shape_all = (STEPS, 2, TOKENS, KV, HD)
    values = jnp.clip(jax.random.normal(draw_key, shape_all, jnp.float32), -6.0, 6.0)
    return values.reshape(STEPS, 2, TOKENS, KV * HD).astype(jnp.bfloat16)


def draw_queries(key, part):
    draw_key = jax.random.fold_in(key, 404)
    group_size = HEADS // KV
    shape_all = (STEPS, TOKENS, KV, group_size, HD)
    values = jnp.clip(jax.random.normal(draw_key, shape_all, jnp.float32), -6.0, 6.0)
    return values.reshape(STEPS, TOKENS, HEADS * HD).astype(jnp.bfloat16)


def draw_logits(key, part):
    draw_key = jax.random.fold_in(key, 505)
    normal_key = jax.random.fold_in(draw_key, 0)
    noise = jax.random.normal(normal_key, (TOKENS, VOCAB), jnp.float32)
    values = jnp.clip(3.0 * noise, -18.0, 18.0)
    return values.astype(jnp.bfloat16)


def plant(entries, key, low, high):
    longest = entries.shape.index(max(entries.shape))
    spots = []
    for shift in (0, 1):
        where = [jax.random.randint(jax.random.fold_in(key, axis), (), 0, length) for axis, length in enumerate(entries.shape)]
        where[longest] = (where[longest] + shift) % entries.shape[longest]
        spots.append(tuple(where))
    return entries.at[spots[0]].set(low).at[spots[1]].set(high)


def setup_inputs(seed: int = 0) -> dict:
    arg_keys = jax.random.split(jax.random.key(seed), 6)
    return {
        "queries": draw_queries(jax.random.fold_in(arg_keys[5], 71), 0),
        "draft_kv": draw_draft_kv(jax.random.fold_in(arg_keys[5], 71), 0),
        "doc_ids": draw_doc_ids(jax.random.fold_in(arg_keys[5], 71), 0),
        "logits": draw_logits(jax.random.fold_in(arg_keys[5], 71), 0),
        "targets": plant(jax.random.randint(arg_keys[4], (TOKENS,), 0, VOCAB), jax.random.fold_in(arg_keys[4], 1), 0, VOCAB - 1).astype(jnp.int32),
    }


negative_fill = -1e30


def attend_step(step_index, queries, draft_kv, doc_ids):
    group_size = HEADS // KV
    block_width = math.gcd(TOKENS, 512)
    score_scale = HD ** -0.5
    query_all = queries[step_index].reshape(TOKENS, KV, group_size, HD)
    key_all = draft_kv[0, 0].reshape(TOKENS, KV, HD)
    value_all = draft_kv[0, 1].reshape(TOKENS, KV, HD)
    diagonal_pairs = [(draft_kv[earlier, 0].reshape(TOKENS, KV, HD), draft_kv[earlier, 1].reshape(TOKENS, KV, HD)) for earlier in range(1, step_index + 1)]

    def one_block(block_index):
        block_start = block_index * block_width
        query_rows = lax.dynamic_slice_in_dim(query_all, block_start, block_width, 0).astype(jnp.float32)
        query_pos = block_start + jnp.arange(block_width, dtype=jnp.int32)
        query_docs = lax.dynamic_slice_in_dim(doc_ids, block_start, block_width, 0)

        def scores_at(key_index):
            key_start = key_index * block_width
            key_rows = lax.dynamic_slice_in_dim(key_all, key_start, block_width, 0).astype(jnp.float32)
            scores = jnp.einsum("tkgd,skd->tkgs", query_rows, key_rows) * score_scale
            key_pos = key_start + jnp.arange(block_width, dtype=jnp.int32)
            key_docs = lax.dynamic_slice_in_dim(doc_ids, key_start, block_width, 0)
            usable = (key_pos[None, :] <= query_pos[:, None]) & (key_docs[None, :] == query_docs[:, None])
            return scores, usable[:, None, None, :], key_start

        def take_max(key_index, highest):
            scores, usable, key_start = scores_at(key_index)
            return jnp.maximum(highest, jnp.max(jnp.where(usable, scores, negative_fill), axis=3))

        row_peak = lax.fori_loop(0, block_index + 1, take_max, jnp.full((block_width, KV, group_size), negative_fill, jnp.float32))
        diagonal_scores = []
        for diag_keys, diag_values in diagonal_pairs:
            diag_rows = lax.dynamic_slice_in_dim(diag_keys, block_start, block_width, 0).astype(jnp.float32)
            diag_score = jnp.einsum("tkgd,tkd->tkg", query_rows, diag_rows) * score_scale
            diagonal_scores.append(diag_score)
            row_peak = jnp.maximum(row_peak, diag_score)

        def add_terms(key_index, state):
            denominator, accumulated = state
            scores, usable, key_start = scores_at(key_index)
            weights = jnp.where(usable, jnp.exp(scores - row_peak[..., None]), 0.0)
            rounded = lax.optimization_barrier(weights.astype(jnp.bfloat16)).astype(jnp.float32)
            value_rows = lax.dynamic_slice_in_dim(value_all, key_start, block_width, 0).astype(jnp.float32)
            accumulated = accumulated + jnp.einsum("tkgs,skd->tkgd", rounded, value_rows)
            return denominator + jnp.sum(weights, axis=3), accumulated

        start_state = (jnp.zeros((block_width, KV, group_size), jnp.float32), jnp.zeros((block_width, KV, group_size, HD), jnp.float32))
        denominator, accumulated = lax.fori_loop(0, block_index + 1, add_terms, start_state)
        for diag_score, pair in zip(diagonal_scores, diagonal_pairs):
            diag_weight = jnp.exp(diag_score - row_peak)
            denominator = denominator + diag_weight
            rounded = lax.optimization_barrier(diag_weight.astype(jnp.bfloat16)).astype(jnp.float32)
            diag_vals = lax.dynamic_slice_in_dim(pair[1], block_start, block_width, 0).astype(jnp.float32)
            accumulated = accumulated + rounded[..., None] * diag_vals[:, :, None, :]
        result = (accumulated / denominator[..., None]).astype(jnp.bfloat16)
        return result.reshape(block_width, HEADS * HD), row_peak.reshape(block_width, HEADS)

    blocks, peaks = lax.map(one_block, jnp.arange(TOKENS // block_width, dtype=jnp.int32))
    return blocks.reshape(TOKENS, HEADS * HD), peaks.reshape(TOKENS, HEADS)


def reference(queries, draft_kv, doc_ids, logits, targets):
    results = [attend_step(step_index, queries, draft_kv, doc_ids) for step_index in range(STEPS)]
    attended = jnp.stack([pair[0] for pair in results])
    row_peak = jnp.stack([pair[1] for pair in results])
    block_width = math.gcd(TOKENS, 512)

    def loss_block(block_index):
        block_start = block_index * block_width
        values = lax.dynamic_slice_in_dim(logits, block_start, block_width, 0).astype(jnp.float32)
        wanted = lax.dynamic_slice_in_dim(targets, block_start, block_width, 0)
        vocab_peak = jnp.max(values, axis=1)
        vocab_total = jnp.sum(jnp.exp(values - vocab_peak[:, None]), axis=1)
        columns = jnp.arange(VOCAB, dtype=jnp.int32)
        target_logit = jnp.sum(jnp.where(columns[None, :] == wanted[:, None], values, 0.0), axis=1)
        return vocab_peak + jnp.log(vocab_total) - target_logit

    token_loss = lax.map(loss_block, jnp.arange(TOKENS // block_width, dtype=jnp.int32)).reshape(TOKENS)
    return attended, row_peak, token_loss
```

```python
import functools

import jax
import jax.numpy as jnp
from jax import lax
from jax.experimental import pallas as pl
from jax.experimental.pallas import tpu as pltpu
from jax.sharding import PartitionSpec as P

HD = 128
SUB = 16
LOG2E = 1.4426950408889634
FILL = -1e30
NT = (((1,), (1,)), ((), ()))
TILE = 2
F32 = jnp.float32
BF16 = jnp.bfloat16


def pack_kernel(kvl, rows, kv_ref, doc_ref, *out_refs):
    chunks = rows // HD
    for k in range(kvl):
        out_ref = out_refs[k]
        cols = slice(k * HD, (k + 1) * HD)
        out_ref[0, 0:rows, :] = kv_ref[0, 0, :, cols]
        vt = kv_ref[0, 1, :, cols].astype(F32).T.astype(BF16)
        docs = doc_ref[...].astype(F32).astype(BF16)
        for h in range(chunks):
            out_ref[0, rows + h * HD : rows + (h + 1) * HD, :] = vt[:, h * HD : (h + 1) * HD]
            out_ref[0, 2 * rows + h * SUB : 2 * rows + (h + 1) * SUB, :] = jnp.broadcast_to(
                docs[:, h * HD : (h + 1) * HD], (SUB, HD)
            )


def pack(draft_kv, doc_ids):
    rows = doc_ids.shape[0]
    kvl = draft_kv.shape[3] // HD
    depth = 2 * rows + SUB * (rows // HD)
    return pl.pallas_call(
        functools.partial(pack_kernel, kvl, rows),
        grid=(1,),
        out_shape=[jax.ShapeDtypeStruct((1, depth, HD), BF16)] * kvl,
        in_specs=[
            pl.BlockSpec((1, 2, rows, kvl * HD), lambda i: (0, 0, 0, 0)),
            pl.BlockSpec((1, rows), lambda i: (0, 0)),
        ],
        out_specs=[pl.BlockSpec((1, depth, HD), lambda i: (0, 0, 0))] * kvl,
        name="pack",
    )(draft_kv, doc_ids.reshape(1, rows))


def attend_kernel(group, rows, shards, steps, chained, scal_ref, q_ref, own_ref, lst_ref, wide_ref, *rest):
    if chained:
        rest = rest[1:]
    out_ref, peak_ref, acc_ref, top_ref, vdt_ref = rest
    step = pl.program_id(0)
    me = scal_ref[0]
    first_doc = scal_ref[1].astype(F32)
    scale = HD ** (-0.5)
    c2 = scale * LOG2E
    chunks = rows // HD

    before = jnp.zeros((SUB, HD), F32)
    for j in range(shards):
        for h in range(chunks):
            docs = wide_ref[j, 2 * rows + h * SUB : 2 * rows + (h + 1) * SUB, :].astype(F32)
            before = before + jnp.where(docs < first_doc, 1.0, 0.0)
    kstart = (jnp.sum(before) * (1.0 / SUB)).astype(jnp.int32)
    lead = lst_ref[...] == 0

    def values(j):
        parts = [wide_ref[j, rows + h * HD : rows + (h + 1) * HD, :] for h in range(chunks)]
        return jnp.concatenate(parts, axis=1)

    def with_ones(vt):
        return jnp.concatenate([vt, jnp.ones((SUB, vt.shape[1]), BF16)], axis=0)

    def query(g):
        return q_ref[0, :, g * HD : (g + 1) * HD]

    key_at = lax.broadcasted_iota(jnp.int32, (rows, rows), 0)
    tok_at = lax.broadcasted_iota(jnp.int32, (rows, rows), 1)
    usable = (key_at <= tok_at) & (key_at >= lst_ref[...])
    own_keys = wide_ref[me, 0:rows, :]
    own_vals = with_ones(values(me))
    for g in range(group):
        s = lax.dot_general(own_keys, query(g), NT, preferred_element_type=F32)
        s = jnp.where(usable, s, FILL)
        top = jnp.max(s, axis=0, keepdims=True)
        p = jnp.exp2((s - top) * c2).astype(BF16)
        acc_ref[g] = jnp.dot(own_vals, p, preferred_element_type=F32)
        top_ref[g : g + 1, :] = top

    def visit(base, count, masked):
        kt = jnp.concatenate([wide_ref[base + b, 0:rows, :] for b in range(count)], axis=0)
        vt = with_ones(jnp.concatenate([values(base + b) for b in range(count)], axis=1))
        if masked:
            key_pos = base * rows + lax.broadcasted_iota(jnp.int32, (count * rows, rows), 0)
            ok = key_pos >= kstart
        for g in range(group):
            s = lax.dot_general(kt, query(g), NT, preferred_element_type=F32)
            if masked:
                s = jnp.where(ok, s, FILL)
            old = top_ref[g : g + 1, :]
            top = jnp.where(lead, jnp.maximum(old, jnp.max(s, axis=0, keepdims=True)), old)
            shift = jnp.where(lead, top, -FILL)
            fade = jnp.exp2((old - top) * c2)
            p = jnp.exp2((s - shift) * c2).astype(BF16)
            acc_ref[g] = acc_ref[g] * fade + jnp.dot(vt, p, preferred_element_type=F32)
            top_ref[g : g + 1, :] = top

    ahead = jnp.maximum(me * rows - kstart, 0)
    whole = ahead // (TILE * rows)
    left = ahead - whole * (TILE * rows)

    @pl.loop(0, whole)
    def _(t):
        visit(me - (t + 1) * TILE, TILE, False)

    for count in range(1, TILE + 1):

        @pl.when((left > (count - 1) * rows) & (left <= count * rows))
        def _():
            visit(me - whole * TILE - count, count, True)

    for i in range(1, steps):

        @pl.when(step == 0)
        def _():
            vdt_ref[i - 1] = own_ref[i, 1].astype(F32).T

        @pl.when(step >= i)
        def _():
            own_key = own_ref[i, 0].astype(F32)
            ones = jnp.ones((SUB, HD), BF16)
            own_val = vdt_ref[i - 1]
            for g in range(group):
                prod = query(g).astype(F32) * own_key
                high = prod.astype(BF16)
                low = (prod - high.astype(F32)).astype(BF16)
                s = lax.dot_general(ones, high, NT, preferred_element_type=F32)
                s = (s + lax.dot_general(ones, low, NT, preferred_element_type=F32))[0:1]
                old = top_ref[g : g + 1, :]
                top = jnp.maximum(old, s)
                fade = jnp.exp2((old - top) * c2)
                w = jnp.exp2((s - top) * c2)
                acc_ref[g, 0:HD] = acc_ref[g, 0:HD] * fade + own_val * w.astype(BF16).astype(F32)
                acc_ref[g, HD : HD + 8] = acc_ref[g, HD : HD + 8] * fade + w
                top_ref[g : g + 1, :] = top

    for g in range(group):
        o = acc_ref[g, 0:HD] / acc_ref[g, HD : HD + 1]
        out_ref[0, :, g * HD : (g + 1) * HD] = o.T.astype(BF16)
    peak_ref[0] = top_ref[0:group] * scale


def attend(k, scal, queries, draft_kv, lstart, wide, out):
    steps, rows, width = queries.shape
    kvl = draft_kv.shape[3] // HD
    group = width // HD // kvl
    shards, depth, _ = wide.shape
    grid_spec = pltpu.PrefetchScalarGridSpec(
        num_scalar_prefetch=1,
        grid=(steps,),
        in_specs=[
            pl.BlockSpec((1, rows, group * HD), lambda j, s: (j, 0, k)),
            pl.BlockSpec((steps, 2, rows, HD), lambda j, s: (0, 0, 0, k)),
            pl.BlockSpec((1, rows), lambda j, s: (0, 0)),
            pl.BlockSpec((shards, depth, HD), lambda j, s: (0, 0, 0)),
        ]
        + ([] if out is None else [pl.BlockSpec(memory_space=pl.ANY)]),
        out_specs=[
            pl.BlockSpec((1, rows, group * HD), lambda j, s: (j, 0, k)),
            pl.BlockSpec((1, group, rows), lambda j, s: (j, 0, 0)),
        ],
        scratch_shapes=[
            pltpu.VMEM((group, HD + SUB, rows), F32),
            pltpu.VMEM((max(group, 8), rows), F32),
            pltpu.VMEM((steps - 1, HD, rows), F32),
        ],
    )
    args = (scal, queries, draft_kv, lstart, wide) + (() if out is None else (out,))
    return pl.pallas_call(
        functools.partial(attend_kernel, group, rows, shards, steps, out is not None),
        out_shape=[
            jax.ShapeDtypeStruct(queries.shape, BF16),
            jax.ShapeDtypeStruct((steps, group, rows), F32),
        ],
        grid_spec=grid_spec,
        input_output_aliases={} if out is None else {5: 0},
        name=f"attend_{k}",
        compiler_params=pltpu.CompilerParams(vmem_limit_bytes=48 << 20),
        cost_estimate=pl.CostEstimate(
            flops=4 * steps * rows * group * HD * shards * rows // 2,
            transcendentals=steps * rows * group * shards * rows // 2,
            bytes_accessed=wide.size * 2 + 4 * steps * rows * group * HD,
        ),
    )(*args)


def loss_kernel(block, width, tgt_ref, x_ref, top_ref, sum_ref, hit_ref):
    first = pl.program_id(0) * block
    step = min(width, 2048)
    peak = x_ref[:, 0:step]
    for c in range(1, width // step):
        peak = jnp.maximum(peak, x_ref[:, c * step : (c + 1) * step])
    peak = jnp.max(peak.astype(F32), axis=1, keepdims=True)
    total = jnp.zeros((block, 512), F32)
    for c in range(width // 512):
        x = x_ref[:, c * 512 : (c + 1) * 512].astype(F32)
        total = total + jnp.exp2((x - peak) * LOG2E)
    total = jnp.sum(total, axis=1, keepdims=True)
    row_at = lax.broadcasted_iota(jnp.int32, (SUB, HD), 0)
    lane_at = lax.broadcasted_iota(jnp.int32, (SUB, HD), 1)
    for b in range(block // SUB):
        hit = jnp.zeros((SUB, HD), F32)
        for r in range(SUB):
            t = tgt_ref[first + b * SUB + r]
            inside = (t >= 0) & (t < width)
            lane = jnp.where(inside, t, 0)
            start = pl.multiple_of((lane // HD) * HD, HD)
            x = x_ref[b * SUB : (b + 1) * SUB, pl.ds(start, HD)].astype(F32)
            pick = (row_at == r) & (lane_at == lane - start) & inside
            hit = jnp.where(pick, x, hit)
        hit_ref[b * SUB : (b + 1) * SUB, :] = jnp.broadcast_to(
            jnp.sum(hit, axis=1, keepdims=True), (SUB, HD)
        )
    top_ref[...] = jnp.broadcast_to(peak, (block, HD))
    sum_ref[...] = jnp.broadcast_to(total, (block, HD))


def loss_parts(logits, local_targets):
    rows, width = logits.shape
    block = 16
    return pl.pallas_call(
        functools.partial(loss_kernel, block, width),
        grid_spec=pltpu.PrefetchScalarGridSpec(
            num_scalar_prefetch=1,
            grid=(rows // block,),
            in_specs=[pl.BlockSpec((block, width), lambda i, t: (i, 0))],
            out_specs=[pl.BlockSpec((block, HD), lambda i, t: (i, 0))] * 3,
        ),
        out_shape=[jax.ShapeDtypeStruct((rows, HD), F32)] * 3,
        name="loss",
        cost_estimate=pl.CostEstimate(
            flops=4 * logits.size, transcendentals=logits.size, bytes_accessed=2 * logits.size
        ),
    )(local_targets, logits)


def local(queries, draft_kv, doc_ids, logits, targets):
    steps, rows, width = queries.shape
    kvl = draft_kv.shape[3] // HD
    packed = pack(draft_kv, doc_ids)
    wides = []
    for k in range(kvl):
        wides.append(lax.all_gather(packed[k], "seq", axis=0, tiled=True))
    lstart = jnp.sum((doc_ids[:, None] < doc_ids[None, :]).astype(jnp.int32), axis=0)
    scal = jnp.stack([lax.axis_index("seq").astype(jnp.int32), doc_ids[0]])
    top, total, hit = loss_parts(logits, targets - lax.axis_index("vocab") * logits.shape[1])
    parts = jnp.stack([top[:, 0], total[:, 0], hit[:, 0]])
    every = lax.all_gather(parts, "vocab", axis=0)
    out = None
    peaks = []
    for k in range(kvl):
        out, peak = attend(k, scal, queries, draft_kv, lstart.reshape(1, rows), wides[k], out)
        peaks.append(peak)
    peak_rows = jnp.concatenate(peaks, axis=1).transpose(0, 2, 1)
    peak = jnp.max(every[:, 0], axis=0)
    total = jnp.sum(every[:, 1] * jnp.exp(every[:, 0] - peak), axis=0)
    token_loss = peak + jnp.log(total) - jnp.sum(every[:, 2], axis=0)
    return (out, peak_rows, token_loss)


def solution(mesh):
    in_specs = (
        P(None, "seq", "vocab"),
        P(None, None, "seq", "vocab"),
        P("seq"),
        P("seq", "vocab"),
        P("seq"),
    )
    out_specs = (P(None, "seq", "vocab"), P(None, "seq", "vocab"), P("seq"))
    return jax.shard_map(local, mesh=mesh, in_specs=in_specs, out_specs=out_specs, check_vma=False)
```

```python
import functools

import jax
import jax.numpy as jnp
from jax import lax
from jax.experimental import pallas as pl
from jax.experimental.pallas import tpu as pltpu
from jax.sharding import PartitionSpec as P

HD = 128
SUB = 16
LOG2E = 1.4426950408889634
FILL = -1e30
NT = (((1,), (1,)), ((), ()))
LIMIT = 100.0
KEEP = HD + 8
F32 = jnp.float32
BF16 = jnp.bfloat16


def pack_kernel(kvl, rows, kv_ref, doc_ref, out_ref):
    chunks = rows // HD
    for k in range(kvl):
        cols = slice(k * HD, (k + 1) * HD)
        out_ref[k, 0:rows, :] = kv_ref[0, 0, :, cols]
        vt = kv_ref[0, 1, :, cols].astype(F32).T.astype(BF16)
        docs = doc_ref[...].astype(F32).astype(BF16)
        for h in range(chunks):
            out_ref[k, rows + h * HD : rows + (h + 1) * HD, :] = vt[:, h * HD : (h + 1) * HD]
            out_ref[k, 2 * rows + h * SUB : 2 * rows + (h + 1) * SUB, :] = jnp.broadcast_to(
                docs[:, h * HD : (h + 1) * HD], (SUB, HD)
            )


def pack(draft_kv, doc_ids):
    rows = doc_ids.shape[0]
    kvl = draft_kv.shape[3] // HD
    depth = 2 * rows + SUB * (rows // HD)
    return pl.pallas_call(
        functools.partial(pack_kernel, kvl, rows),
        grid=(1,),
        out_shape=jax.ShapeDtypeStruct((kvl, depth, HD), BF16),
        in_specs=[
            pl.BlockSpec((1, 2, rows, kvl * HD), lambda i: (0, 0, 0, 0)),
            pl.BlockSpec((1, rows), lambda i: (0, 0)),
        ],
        out_specs=pl.BlockSpec((kvl, depth, HD), lambda i: (0, 0, 0)),
        name="pack",
    )(draft_kv, doc_ids.reshape(1, rows))


def stage_kernel(group, rows, steps, pairs, first, last, scal_ref, *refs):
    refs = list(refs)
    q_refs = [refs.pop(0) for _ in range(group)]
    blocks = [refs.pop(0) for _ in range(2 * pairs)]
    lst_ref = refs.pop(0)
    if first:
        own_ref = refs.pop(0)
    else:
        acc_in = refs.pop(0)
        top_in = refs.pop(0)
    if last:
        out_ref, peak_ref, acc_out, top_out, count_ref, flag_ref = refs
    elif first:
        acc_out, top_out, own_s, count_ref, flag_ref = refs
    else:
        acc_out, top_out, count_ref, flag_ref = refs
    step = pl.program_id(1)
    scale = HD ** (-0.5)
    c2 = scale * LOG2E
    chunks = rows // HD
    lead = lst_ref[...] == 0

    @pl.when((pl.program_id(0) == 0) & (step == 0))
    def _():
        first_doc = scal_ref[0].astype(F32)
        for b in range(2 * pairs):
            below = jnp.zeros((SUB, HD), F32)
            for h in range(chunks):
                docs = blocks[b][0, 2 * rows + h * SUB : 2 * rows + (h + 1) * SUB, :].astype(F32)
                below = below + jnp.where(docs < first_doc, 1.0, 0.0)
            below = (jnp.sum(below) * (1.0 / SUB)).astype(jnp.int32)
            count_ref[b] = jnp.where(scal_ref[1 + b] == 1, below, rows)

    def values(b):
        parts = [blocks[b][0, rows + h * HD : rows + (h + 1) * HD, :] for h in range(chunks)]
        return jnp.concatenate([jnp.concatenate(parts, axis=1), jnp.ones((SUB, rows), BF16)], axis=0)

    def visit(pair, masked, fresh):
        pick = (2 * pair, 2 * pair + 1)
        vt = jnp.concatenate([values(b) for b in pick], axis=1)
        if masked:
            key_at = lax.broadcasted_iota(jnp.int32, (rows, rows), 0)
            ok = [key_at >= count_ref[b] for b in pick]
            if first:
                tok_at = lax.broadcasted_iota(jnp.int32, (rows, rows), 1)
                ok[0] = (key_at <= tok_at) & (key_at >= lst_ref[...])
                ok[1] = ok[1] & (lst_ref[...] == 0)
        waiting = []
        for g in range(group + 2):
            if g < group:
                ref = top_out[0, 0, g : g + 1, :]
                shift = (ref if first else jnp.where(lead, ref, -FILL)) * c2
                best = None
                probs = []
                for i, b in enumerate(pick):
                    s = lax.dot_general(
                        blocks[b][0, 0:rows, :], q_refs[g][0], NT, preferred_element_type=F32
                    )
                    if masked:
                        s = jnp.where(ok[i], s, FILL)
                    m = jnp.max(s.reshape(rows // 8, 8, rows), axis=0)
                    best = m if best is None else jnp.maximum(best, m)
                    probs.append(jnp.exp2(s * c2 - shift).astype(BF16))
                best = jnp.max(best, axis=0, keepdims=True)
                if not first:
                    best = jnp.where(lead, best, FILL)
                top_out[0, 1, g : g + 1, :] = jnp.maximum(top_out[0, 1, g : g + 1, :], best)
                waiting.append((g, jnp.concatenate(probs, axis=0)))
            if g >= 2:
                w, p = waiting.pop(0)
                more = jnp.dot(vt, p, preferred_element_type=F32)[0:KEEP]
                if fresh:
                    acc_out[0, w] = acc_in[0, w] * top_out[0, 2, w : w + 1, :] + more
                else:
                    acc_out[0, w] = acc_out[0, w] + more

    def carry_over():
        for g in range(group):
            acc_out[0, g] = acc_in[0, g] * top_out[0, 2, g : g + 1, :]

    if first:

        ones = jnp.ones((SUB, HD), BF16)

        def diagonal(g, i):
            prod = q_refs[g][0].astype(F32) * own_ref[i, 0].astype(F32)
            high = prod.astype(BF16)
            low = (prod - high.astype(F32)).astype(BF16)
            both = jnp.concatenate([high, low], axis=1)
            wide = jnp.concatenate([ones, ones], axis=1)
            return lax.dot_general(wide, both, NT, preferred_element_type=F32)[0:1]

        for i in range(steps):

            @pl.when(step >= i)
            def _():
                for g in range(group):
                    own_s[i, g : g + 1, :] = diagonal(g, i)

            @pl.when(step < i)
            def _():
                own_s[i] = jnp.full((group, rows), FILL, F32)

        top_out[0, 0] = functools.reduce(jnp.maximum, [own_s[i] for i in range(steps)])
        top_out[0, 1] = top_out[0, 0]

        def start():
            weights = [jnp.exp2((own_s[i] - top_out[0, 0]) * c2) for i in range(1, steps)]
            for g in range(group):
                acc_out[0, g, 0:HD] = jnp.zeros((HD, rows), F32)
                acc_out[0, g, HD:KEEP] = jnp.broadcast_to(
                    functools.reduce(jnp.add, weights)[g : g + 1, :], (KEEP - HD, rows)
                )
            for i in range(1, steps):

                @pl.when(step >= i)
                def _():
                    own_val = own_ref[i, 1].astype(F32).T
                    for g in range(group):
                        w = weights[i - 1][g : g + 1, :].astype(BF16).astype(F32)
                        acc_out[0, g, 0:HD] = acc_out[0, g, 0:HD] + own_val * w

    else:
        top_out[0, 0] = top_in[0, 0]
        top_out[0, 1] = top_in[0, 1]
        top_out[0, 2] = jnp.ones((group, rows), F32)

    flag_ref[0] = 1

    @pl.loop(0, 2)
    def _(_):
        @pl.when(flag_ref[0] == 1)
        def _():
            if first:
                start()
                visit(0, True, False)
            else:
                for pair in range(pairs):
                    a, b = count_ref[2 * pair], count_ref[2 * pair + 1]
                    some = jnp.minimum(a, b) < rows
                    full = jnp.maximum(a, b) == 0

                    @pl.when(full)
                    def _():
                        visit(pair, False, pair == 0)

                    @pl.when(some & jnp.logical_not(full))
                    def _():
                        visit(pair, True, pair == 0)

                    if pair == 0:

                        @pl.when(jnp.logical_not(some))
                        def _():
                            carry_over()

            over = jnp.max(top_out[0, 1] - top_out[0, 0]) * c2 > LIMIT
            flag_ref[0] = over.astype(jnp.int32)

            @pl.when(over)
            def _():
                top_out[0, 2] = jnp.exp2((top_out[0, 0] - top_out[0, 1]) * c2)
                top_out[0, 0] = top_out[0, 1]

    if last:
        for g in range(group):
            o = acc_out[0, g, 0:HD] / acc_out[0, g, HD : HD + 1]
            out_ref[0, :, g * HD : (g + 1) * HD] = o.T.astype(BF16)
        peak_ref[0] = top_out[0, 1] * scale


def stage(queries, draft_kv, blocks, lstart, scal, state, last):
    steps, rows, width = queries.shape
    kvl = draft_kv.shape[3] // HD
    group = width // HD // kvl
    depth = blocks[0].shape[1]
    first = state is None
    pairs = len(blocks) // 2
    q_specs = [
        pl.BlockSpec((1, rows, HD), functools.partial(lambda g, k, j, s: (j, 0, k * group + g), g))
        for g in range(group)
    ]
    acc_shape = (kvl * steps, group, KEEP, rows)
    top_shape = (kvl * steps, 3, group, rows)
    acc_spec = pl.BlockSpec((1, group, KEEP, rows), lambda k, j, s: (k * steps + j, 0, 0, 0))
    top_spec = pl.BlockSpec((1, 3, group, rows), lambda k, j, s: (k * steps + j, 0, 0, 0))
    own_spec = pl.BlockSpec((steps, 2, rows, HD), lambda k, j, s: (0, 0, 0, k))
    in_specs = (
        q_specs
        + [pl.BlockSpec((1, depth, HD), lambda k, j, s: (k, 0, 0))] * len(blocks)
        + [pl.BlockSpec((1, rows), lambda k, j, s: (0, 0))]
        + ([own_spec] if first else [acc_spec, top_spec])
    )
    args = [queries] * group + blocks + [lstart] + ([draft_kv] if first else list(state))
    scratch = [pltpu.SMEM((2 * pairs,), jnp.int32), pltpu.SMEM((1,), jnp.int32)]
    if first:
        scratch = [pltpu.VMEM((steps, group, rows), F32)] + scratch
    if last:
        out_shape = [
            jax.ShapeDtypeStruct(queries.shape, BF16),
            jax.ShapeDtypeStruct((steps, kvl * group, rows), F32),
        ]
        out_specs = [
            pl.BlockSpec((1, rows, group * HD), lambda k, j, s: (j, 0, k)),
            pl.BlockSpec((1, group, rows), lambda k, j, s: (j, k, 0)),
        ]
        scratch = [
            pltpu.VMEM((1, group, KEEP, rows), F32),
            pltpu.VMEM((1, 3, group, rows), F32),
        ] + scratch
        aliases = {}
    else:
        out_shape = [jax.ShapeDtypeStruct(acc_shape, F32), jax.ShapeDtypeStruct(top_shape, F32)]
        out_specs = [acc_spec, top_spec]
        aliases = {} if first else {len(args) - 1: 0, len(args): 1}
    work = kvl * steps * group * rows * rows * len(blocks)
    return pl.pallas_call(
        functools.partial(stage_kernel, group, rows, steps, pairs, first, last),
        out_shape=out_shape,
        grid_spec=pltpu.PrefetchScalarGridSpec(
            num_scalar_prefetch=1,
            grid=(kvl, steps),
            in_specs=in_specs,
            out_specs=out_specs,
            scratch_shapes=scratch,
        ),
        input_output_aliases=aliases,
        name="stage_first" if first else ("stage_last" if last else "stage_mid"),
        compiler_params=pltpu.CompilerParams(vmem_limit_bytes=40 << 20),
        cost_estimate=pl.CostEstimate(
            flops=4 * work * HD, transcendentals=work, bytes_accessed=4 * kvl * steps * group * HD * rows
        ),
    )(scal, *args)


def loss_kernel(block, width, tgt_ref, x_ref, top_ref, sum_ref, hit_ref):
    first = pl.program_id(0) * block
    step = min(width, 2048)
    peak = x_ref[:, 0:step]
    for c in range(1, width // step):
        peak = jnp.maximum(peak, x_ref[:, c * step : (c + 1) * step])
    peak = jnp.max(peak.astype(F32), axis=1, keepdims=True)
    total = jnp.zeros((block, 512), F32)
    for c in range(width // 512):
        x = x_ref[:, c * 512 : (c + 1) * 512].astype(F32)
        total = total + jnp.exp2((x - peak) * LOG2E)
    total = jnp.sum(total, axis=1, keepdims=True)
    row_at = lax.broadcasted_iota(jnp.int32, (SUB, HD), 0)
    lane_at = lax.broadcasted_iota(jnp.int32, (SUB, HD), 1)
    for b in range(block // SUB):
        hit = jnp.zeros((SUB, HD), F32)
        for r in range(SUB):
            t = tgt_ref[first + b * SUB + r]
            inside = (t >= 0) & (t < width)
            lane = jnp.where(inside, t, 0)
            start = pl.multiple_of((lane // HD) * HD, HD)
            x = x_ref[b * SUB : (b + 1) * SUB, pl.ds(start, HD)].astype(F32)
            pick = (row_at == r) & (lane_at == lane - start) & inside
            hit = jnp.where(pick, x, hit)
        hit_ref[b * SUB : (b + 1) * SUB, :] = jnp.broadcast_to(
            jnp.sum(hit, axis=1, keepdims=True), (SUB, HD)
        )
    top_ref[...] = jnp.broadcast_to(peak, (block, HD))
    sum_ref[...] = jnp.broadcast_to(total, (block, HD))


def loss_parts(logits, local_targets):
    rows, width = logits.shape
    block = 16
    return pl.pallas_call(
        functools.partial(loss_kernel, block, width),
        grid_spec=pltpu.PrefetchScalarGridSpec(
            num_scalar_prefetch=1,
            grid=(rows // block,),
            in_specs=[pl.BlockSpec((block, width), lambda i, t: (i, 0))],
            out_specs=[pl.BlockSpec((block, HD), lambda i, t: (i, 0))] * 3,
        ),
        out_shape=[jax.ShapeDtypeStruct((rows, HD), F32)] * 3,
        name="loss",
        cost_estimate=pl.CostEstimate(
            flops=4 * logits.size, transcendentals=logits.size, bytes_accessed=2 * logits.size
        ),
    )(local_targets, logits)


def local(queries, draft_kv, doc_ids, logits, targets):
    steps, rows, width = queries.shape
    me = lax.axis_index("seq").astype(jnp.int32)
    shards = lax.axis_size("seq")
    levels = shards // 4
    lstart = jnp.sum((doc_ids[:, None] < doc_ids[None, :]).astype(jnp.int32), axis=0).reshape(1, rows)

    def up(x):
        return lax.ppermute(x, "seq", [(i, i + 4) for i in range(shards - 4)])

    def swap(x, bit):
        return lax.ppermute(x, "seq", [(i, i ^ bit) for i in range(shards)])

    def scalars(sources):
        earlier = [((s >= 0) & (s < me)).astype(jnp.int32) for s in sources]
        return jnp.stack([doc_ids[0]] + earlier)

    def place(flip, level):
        return (me ^ flip) - 4 * level

    mine = pack(draft_kv, doc_ids)
    z, x, c, d = [mine], [], [], []
    z.append(up(z[0]))
    x.append(swap(z[0], 2))
    c.append(swap(z[0], 1))
    top, total, hit = loss_parts(logits, targets - lax.axis_index("vocab") * logits.shape[1])
    parts = jnp.stack([top[:, 0], total[:, 0], hit[:, 0]])
    every = lax.all_gather(parts, "vocab", axis=0)
    for level in range(1, levels):
        if level + 1 < levels:
            z.append(up(z[level]))
        x.append(swap(z[level], 2))
        c.append(swap(z[level], 1))
        d.append(swap(x[level - 1], 1))
    d.append(swap(x[levels - 1], 1))
    state = stage(queries, draft_kv, [z[0], c[0]], lstart, scalars([me, place(1, 0)]), None, False)
    for level in range(1, levels):
        blocks = [z[level], c[level], x[level - 1], d[level - 1]]
        sources = [place(0, level), place(1, level), place(2, level - 1), place(3, level - 1)]
        state = stage(queries, draft_kv, blocks, lstart, scalars(sources), state, False)
    sources = [place(2, levels - 1), place(3, levels - 1)]
    out, peaks = stage(
        queries, draft_kv, [x[levels - 1], d[levels - 1]], lstart, scalars(sources), state, True
    )
    peak = jnp.max(every[:, 0], axis=0)
    total = jnp.sum(every[:, 1] * jnp.exp(every[:, 0] - peak), axis=0)
    token_loss = peak + jnp.log(total) - jnp.sum(every[:, 2], axis=0)
    return (out, peaks.transpose(0, 2, 1), token_loss)


def solution(mesh):
    in_specs = (
        P(None, "seq", "vocab"),
        P(None, None, "seq", "vocab"),
        P("seq"),
        P("seq", "vocab"),
        P("seq"),
    )
    out_specs = (P(None, "seq", "vocab"), P(None, "seq", "vocab"), P("seq"))
    return jax.shard_map(local, mesh=mesh, in_specs=in_specs, out_specs=out_specs, check_vma=False)
```

```python
import functools

import jax
import jax.numpy as jnp
from jax import lax
from jax.experimental import pallas as pl
from jax.experimental.pallas import tpu as pltpu
from jax.sharding import PartitionSpec as P

HD = 128
SUB = 16
LOG2E = 1.4426950408889634
FILL = -1e30
NT = (((1,), (1,)), ((), ()))
LIMIT = 100.0
KEEP = HD + 8
VMEM = 60 << 20
F32 = jnp.float32
BF16 = jnp.bfloat16


def pack_kernel(kvl, rows, kv_ref, doc_ref, out_ref, lst_ref):
    chunks = rows // HD
    along = jnp.broadcast_to(doc_ref[...].astype(F32), (rows, rows))
    lst_ref[...] = jnp.sum(jnp.where(along.T < along, 1.0, 0.0), axis=0, keepdims=True)
    for k in range(kvl):
        cols = slice(k * HD, (k + 1) * HD)
        out_ref[k, 0:rows, :] = kv_ref[0, 0, :, cols]
        vt = kv_ref[0, 1, :, cols].astype(F32).T.astype(BF16)
        docs = doc_ref[...].astype(F32).astype(BF16)
        for h in range(chunks):
            out_ref[k, rows + h * HD : rows + (h + 1) * HD, :] = vt[:, h * HD : (h + 1) * HD]
            out_ref[k, 2 * rows + h * SUB : 2 * rows + (h + 1) * SUB, :] = jnp.broadcast_to(
                docs[:, h * HD : (h + 1) * HD], (SUB, HD)
            )


def pack(draft_kv, doc_ids):
    rows = doc_ids.shape[0]
    kvl = draft_kv.shape[3] // HD
    depth = 2 * rows + SUB * (rows // HD)
    return pl.pallas_call(
        functools.partial(pack_kernel, kvl, rows),
        grid=(1,),
        out_shape=[
            jax.ShapeDtypeStruct((kvl, depth, HD), BF16),
            jax.ShapeDtypeStruct((1, rows), F32),
        ],
        in_specs=[
            pl.BlockSpec((1, 2, rows, kvl * HD), lambda i: (0, 0, 0, 0)),
            pl.BlockSpec((1, rows), lambda i: (0, 0)),
        ],
        out_specs=[
            pl.BlockSpec((kvl, depth, HD), lambda i: (0, 0, 0)),
            pl.BlockSpec((1, rows), lambda i: (0, 0)),
        ],
        name="pack",
    )(draft_kv, doc_ids.reshape(1, rows))


def stage_kernel(group, rows, steps, sources, first, last, doc_ref, *refs):
    refs = list(refs)
    pairs = len(sources) // 2
    q_ref = refs.pop(0)
    blocks = [refs.pop(0) for _ in range(2 * pairs)]
    lst_ref = refs.pop(0)
    if first:
        own_ref = refs.pop(0)
    else:
        acc_in = refs.pop(0)
        top_in = refs.pop(0)
    if last:
        loss_ref, out_ref, peak_ref, loss_out, acc_out, top_out, q_all, count_ref, flag_ref = refs
    elif first:
        acc_out, top_out, own_s, q_all, count_ref, flag_ref = refs
    else:
        acc_out, top_out, q_all, count_ref, flag_ref = refs
    step = pl.program_id(1)
    opening = (pl.program_id(0) == 0) & (step == 0)
    scale = HD ** (-0.5)
    c2 = scale * LOG2E
    chunks = rows // HD
    lead = lst_ref[...] == 0.0
    for g in range(group):
        q_all[g] = q_ref[0, :, g * HD : (g + 1) * HD]

    @pl.when(opening)
    def _():
        me = lax.axis_index("seq")
        first_doc = doc_ref[0].astype(F32)
        for b, (flip, level) in enumerate(sources):
            source = (me ^ flip) - 4 * level
            below = jnp.zeros((SUB, HD), F32)
            for h in range(chunks):
                docs = blocks[b][0, 2 * rows + h * SUB : 2 * rows + (h + 1) * SUB, :].astype(F32)
                below = below + jnp.where(docs < first_doc, 1.0, 0.0)
            below = (jnp.sum(below) * (1.0 / SUB)).astype(jnp.int32)
            count_ref[b] = jnp.where((source >= 0) & (source < me), below, rows)

    if last:

        @pl.when(opening)
        def _():
            peak = jnp.max(loss_ref[:, 0:1, :], axis=0)
            total = jnp.sum(loss_ref[:, 1:2, :] * jnp.exp(loss_ref[:, 0:1, :] - peak), axis=0)
            loss_out[...] = peak + jnp.log(total) - jnp.sum(loss_ref[:, 2:3, :], axis=0)

    def values(b):
        parts = [blocks[b][0, rows + h * HD : rows + (h + 1) * HD, :] for h in range(chunks)]
        return jnp.concatenate([jnp.concatenate(parts, axis=1), jnp.ones((SUB, rows), BF16)], axis=0)

    def visit(pair, masked, fresh):
        pick = (2 * pair, 2 * pair + 1)
        vt = jnp.concatenate([values(b) for b in pick], axis=1)
        if masked:
            key_at = lax.broadcasted_iota(jnp.int32, (rows, rows), 0)
            ok = [key_at >= count_ref[b] for b in pick]
            if first:
                tok_at = lax.broadcasted_iota(jnp.int32, (rows, rows), 1)
                ok[0] = (key_at <= tok_at) & (key_at.astype(F32) >= lst_ref[...])
                ok[1] = ok[1] & lead
        waiting = []
        for g in range(group + 2):
            if g < group:
                ref = top_out[0, 0, g : g + 1, :]
                shift = (ref if first else jnp.where(lead, ref, -FILL)) * c2
                best = None
                probs = []
                for i, b in enumerate(pick):
                    s = lax.dot_general(
                        blocks[b][0, 0:rows, :], q_all[g], NT, preferred_element_type=F32
                    )
                    if masked:
                        s = jnp.where(ok[i], s, FILL)
                    m = jnp.max(s.reshape(rows // 8, 8, rows), axis=0)
                    best = m if best is None else jnp.maximum(best, m)
                    probs.append(jnp.exp2(s * c2 - shift).astype(BF16))
                best = jnp.max(best, axis=0, keepdims=True)
                if not first:
                    best = jnp.where(lead, best, FILL)
                top_out[0, 1, g : g + 1, :] = jnp.maximum(top_out[0, 1, g : g + 1, :], best)
                waiting.append((g, jnp.concatenate(probs, axis=0)))
            if g >= 2:
                w, p = waiting.pop(0)
                more = jnp.dot(vt, p, preferred_element_type=F32)[0:KEEP]
                if fresh:
                    acc_out[0, w] = acc_in[0, w] * top_out[0, 2, w : w + 1, :] + more
                else:
                    acc_out[0, w] = acc_out[0, w] + more

    def carry_over():
        for g in range(group):
            acc_out[0, g] = acc_in[0, g] * top_out[0, 2, g : g + 1, :]

    if first:

        ones = jnp.ones((SUB, HD), BF16)

        def diagonal(g, i):
            prod = q_all[g].astype(F32) * own_ref[i, 0].astype(F32)
            high = prod.astype(BF16)
            low = (prod - high.astype(F32)).astype(BF16)
            both = jnp.concatenate([high, low], axis=1)
            wide = jnp.concatenate([ones, ones], axis=1)
            return lax.dot_general(wide, both, NT, preferred_element_type=F32)[0:1]

        for i in range(1, steps):

            @pl.when(step >= i)
            def _():
                for g in range(group):
                    own_s[i, g : g + 1, :] = diagonal(g, i)

            @pl.when(step < i)
            def _():
                own_s[i] = jnp.full((group, rows), FILL, F32)

        for g in range(group):
            near = q_all[g] * own_ref[0, 0]
            own_s[0, g : g + 1, :] = lax.dot_general(ones, near, NT, preferred_element_type=F32)[0:1]
        top_out[0, 1] = functools.reduce(jnp.maximum, [own_s[i] for i in range(1, steps)])
        top_out[0, 0] = jnp.maximum(top_out[0, 1], own_s[0])

        def start():
            weights = [jnp.exp2((own_s[i] - top_out[0, 0]) * c2) for i in range(1, steps)]
            for g in range(group):
                acc_out[0, g, 0:HD] = jnp.zeros((HD, rows), F32)
                acc_out[0, g, HD:KEEP] = jnp.broadcast_to(
                    functools.reduce(jnp.add, weights)[g : g + 1, :], (KEEP - HD, rows)
                )
            for i in range(1, steps):

                @pl.when(step >= i)
                def _():
                    own_val = own_ref[i, 1].astype(F32).T
                    for g in range(group):
                        w = weights[i - 1][g : g + 1, :].astype(BF16).astype(F32)
                        acc_out[0, g, 0:HD] = acc_out[0, g, 0:HD] + own_val * w

    else:
        top_out[0, 0] = top_in[0, 0]
        top_out[0, 1] = top_in[0, 1]
        top_out[0, 2] = jnp.ones((group, rows), F32)

    flag_ref[0] = 1

    @pl.loop(0, 2)
    def _(_):
        @pl.when(flag_ref[0] == 1)
        def _():
            if first:
                start()
                visit(0, True, False)
            else:
                for pair in range(pairs):
                    a, b = count_ref[2 * pair], count_ref[2 * pair + 1]
                    some = jnp.minimum(a, b) < rows
                    full = jnp.maximum(a, b) == 0

                    @pl.when(full)
                    def _():
                        visit(pair, False, pair == 0)

                    @pl.when(some & jnp.logical_not(full))
                    def _():
                        visit(pair, True, pair == 0)

                    if pair == 0:

                        @pl.when(jnp.logical_not(some))
                        def _():
                            carry_over()

            over = jnp.max(top_out[0, 1] - top_out[0, 0]) * c2 > LIMIT
            flag_ref[0] = over.astype(jnp.int32)

            @pl.when(over)
            def _():
                top_out[0, 2] = jnp.exp2((top_out[0, 0] - top_out[0, 1]) * c2)
                top_out[0, 0] = top_out[0, 1]

    if last:
        for g in range(group):
            o = acc_out[0, g, 0:HD] * (1.0 / acc_out[0, g, HD : HD + 1])
            out_ref[0, :, g * HD : (g + 1) * HD] = o.T.astype(BF16)
        peak_ref[0] = top_out[0, 1] * scale


def stage(queries, draft_kv, doc_ids, blocks, lstart, sources, state, losses):
    steps, rows, width = queries.shape
    kvl = draft_kv.shape[3] // HD
    group = width // HD // kvl
    depth = blocks[0].shape[1]
    first = state is None
    last = losses is not None
    acc_shape = (kvl * steps, group, KEEP, rows)
    top_shape = (kvl * steps, 3, group, rows)
    acc_spec = pl.BlockSpec((1, group, KEEP, rows), lambda k, j, s: (k * steps + j, 0, 0, 0))
    top_spec = pl.BlockSpec((1, 3, group, rows), lambda k, j, s: (k * steps + j, 0, 0, 0))
    row_spec = pl.BlockSpec((1, rows), lambda k, j, s: (0, 0))
    in_specs = (
        [pl.BlockSpec((1, rows, group * HD), lambda k, j, s: (j, 0, k))]
        + [pl.BlockSpec((1, depth, HD), lambda k, j, s: (k, 0, 0))] * len(blocks)
        + [row_spec]
    )
    args = [queries] + blocks + [lstart]
    scratch = [
        pltpu.VMEM((group, rows, HD), BF16),
        pltpu.SMEM((len(blocks),), jnp.int32),
        pltpu.SMEM((1,), jnp.int32),
    ]
    aliases = {}
    out_shape = [jax.ShapeDtypeStruct(acc_shape, F32), jax.ShapeDtypeStruct(top_shape, F32)]
    out_specs = [acc_spec, top_spec]
    if first:
        args += [draft_kv]
        in_specs += [pl.BlockSpec((steps, 2, rows, HD), lambda k, j, s: (0, 0, 0, k))]
        scratch = [pltpu.VMEM((steps, group, rows), F32)] + scratch
    else:
        aliases = {len(args) + 1: 0, len(args) + 2: 1}
        args += list(state)
        in_specs += [acc_spec, top_spec]
    if last:
        aliases = {}
        args += [losses]
        in_specs += [pl.BlockSpec(losses.shape, lambda k, j, s: (0, 0, 0))]
        out_shape = [
            jax.ShapeDtypeStruct(queries.shape, BF16),
            jax.ShapeDtypeStruct((steps, kvl * group, rows), F32),
            jax.ShapeDtypeStruct((1, rows), F32),
        ]
        out_specs = [
            pl.BlockSpec((1, rows, group * HD), lambda k, j, s: (j, 0, k)),
            pl.BlockSpec((1, group, rows), lambda k, j, s: (j, k, 0)),
            row_spec,
        ]
        scratch = [
            pltpu.VMEM((1, group, KEEP, rows), F32),
            pltpu.VMEM((1, 3, group, rows), F32),
        ] + scratch
    work = kvl * steps * group * rows * rows * len(blocks)
    return pl.pallas_call(
        functools.partial(stage_kernel, group, rows, steps, sources, first, last),
        out_shape=out_shape,
        grid_spec=pltpu.PrefetchScalarGridSpec(
            num_scalar_prefetch=1,
            grid=(kvl, steps),
            in_specs=in_specs,
            out_specs=out_specs,
            scratch_shapes=scratch,
        ),
        input_output_aliases=aliases,
        name="stage_first" if first else ("stage_last" if last else "stage_mid"),
        compiler_params=pltpu.CompilerParams(vmem_limit_bytes=VMEM),
        cost_estimate=pl.CostEstimate(
            flops=4 * work * HD, transcendentals=work, bytes_accessed=4 * kvl * steps * group * HD * rows
        ),
    )(doc_ids, *args)


def loss_kernel(block, width, tgt_ref, x_ref, out_ref, all_ref):
    i = pl.program_id(0)
    first = i * block
    start_col = lax.axis_index("vocab") * width
    step = min(width, 2048)
    wide = min(width, 512)
    row_at = lax.broadcasted_iota(jnp.int32, (SUB, HD), 0)
    lane_at = lax.broadcasted_iota(jnp.int32, (SUB, HD), 1)

    @pl.loop(0, block // SUB)
    def _(b):
        here = pl.ds(pl.multiple_of(b * SUB, SUB), SUB)
        peak = x_ref[here, 0:step]
        for c in range(1, width // step):
            peak = jnp.maximum(peak, x_ref[here, c * step : (c + 1) * step])
        peak = jnp.max(peak.astype(F32), axis=1, keepdims=True)
        total = jnp.zeros((SUB, wide), F32)
        for c in range(width // wide):
            x = x_ref[here, c * wide : (c + 1) * wide].astype(F32)
            total = total + jnp.exp2((x - peak) * LOG2E)
        total = jnp.sum(total, axis=1, keepdims=True)
        hit = jnp.zeros((SUB, HD), F32)
        for r in range(SUB):
            t = tgt_ref[first + b * SUB + r] - start_col
            inside = (t >= 0) & (t < width)
            lane = jnp.where(inside, t, 0)
            start = pl.multiple_of((lane // HD) * HD, HD)
            x = x_ref[here, pl.ds(start, HD)].astype(F32)
            hit = jnp.where((row_at == r) & (lane_at == lane - start) & inside, x, hit)
        hit = jnp.sum(hit, axis=1, keepdims=True)
        there = pl.ds(pl.multiple_of(first + b * SUB, SUB), SUB)
        all_ref[there, :] = jnp.where(lane_at == 0, peak, jnp.where(lane_at == 1, total, hit))

    @pl.when(i == pl.num_programs(0) - 1)
    def _():
        out_ref[0] = all_ref[...].T[0:8]


def loss_parts(logits, targets):
    rows, width = logits.shape
    block = 64
    return pl.pallas_call(
        functools.partial(loss_kernel, block, width),
        grid_spec=pltpu.PrefetchScalarGridSpec(
            num_scalar_prefetch=1,
            grid=(rows // block,),
            in_specs=[pl.BlockSpec((block, width), lambda i, t: (i, 0))],
            out_specs=pl.BlockSpec((1, 8, rows), lambda i, t: (0, 0, 0)),
            scratch_shapes=[pltpu.VMEM((rows, HD), F32)],
        ),
        out_shape=jax.ShapeDtypeStruct((1, 8, rows), F32),
        name="loss",
        compiler_params=pltpu.CompilerParams(vmem_limit_bytes=VMEM),
        cost_estimate=pl.CostEstimate(
            flops=4 * logits.size, transcendentals=logits.size, bytes_accessed=2 * logits.size
        ),
    )(targets, logits)


def local(queries, draft_kv, doc_ids, logits, targets):
    shards = lax.axis_size("seq")
    halves = lax.axis_size("vocab")
    levels = shards // 4

    def up(x):
        return lax.ppermute(x, "seq", [(i, i + 4) for i in range(shards - 4)])

    def swap(x, bit):
        return lax.ppermute(x, "seq", [(i, i ^ bit) for i in range(shards)])

    mine, lstart = pack(draft_kv, doc_ids)
    z, x, c, d = [mine], [], [], []
    z.append(up(z[0]))
    x.append(swap(z[0], 2))
    c.append(swap(z[0], 1))
    parts = loss_parts(logits, targets)
    turns = [
        lax.ppermute(parts, "vocab", [(i, (i + t) % halves) for i in range(halves)])
        for t in range(1, halves)
    ]
    for level in range(1, levels):
        if level + 1 < levels:
            z.append(up(z[level]))
        x.append(swap(z[level], 2))
        c.append(swap(z[level], 1))
        d.append(swap(x[level - 1], 1))
    d.append(swap(x[levels - 1], 1))

    def run(blocks, sources, state, losses=None):
        return stage(queries, draft_kv, doc_ids, blocks, lstart, sources, state, losses)

    state = run([z[0], c[0]], [(0, 0), (1, 0)], None)
    for level in range(1, levels):
        blocks = [z[level], c[level], x[level - 1], d[level - 1]]
        state = run(blocks, [(0, level), (1, level), (2, level - 1), (3, level - 1)], state)
    losses = jnp.concatenate([parts] + turns, axis=0)
    final = levels - 1
    out, peaks, token_loss = run([x[final], d[final]], [(2, final), (3, final)], state, losses)
    return (out, peaks.transpose(0, 2, 1), token_loss.reshape(-1))


def solution(mesh):
    in_specs = (
        P(None, "seq", "vocab"),
        P(None, None, "seq", "vocab"),
        P("seq"),
        P("seq", "vocab"),
        P("seq"),
    )
    out_specs = (P(None, "seq", "vocab"), P(None, "seq", "vocab"), P("seq"))
    return jax.shard_map(local, mesh=mesh, in_specs=in_specs, out_specs=out_specs, check_vma=False)
```

```python
import functools

import jax
import jax.numpy as jnp
from jax import lax
from jax.experimental import pallas as pl
from jax.experimental.pallas import tpu as pltpu
from jax.sharding import PartitionSpec as P


HD = 128
SUB = 16
LOG2E = 1.4426950408889634
FILL = -1e30
NT = (((1,), (1,)), ((), ()))
LIMIT = 100.0
KEEP = HD + 8
VMEM = 67043328
F32 = jnp.float32
BF16 = jnp.bfloat16


def pack_kernel(kvl, rows, kv_ref, doc_ref, out_ref, lst_ref):
    chunks = rows // HD
    along = jnp.broadcast_to(doc_ref[...].astype(F32), (rows, rows))
    lst_ref[...] = jnp.sum(jnp.where(along.T < along, 1.0, 0.0), axis=0, keepdims=True)
    for k in range(kvl):
        cols = slice(k * HD, (k + 1) * HD)
        out_ref[k, 0:rows, :] = kv_ref[0, 0, :, cols]
        vt = kv_ref[0, 1, :, cols].astype(F32).T.astype(BF16)
        docs = doc_ref[...].astype(F32).astype(BF16)
        for h in range(chunks):
            out_ref[k, rows + h * HD : rows + (h + 1) * HD, :] = vt[:, h * HD : (h + 1) * HD]
            out_ref[k, 2 * rows + h * SUB : 2 * rows + (h + 1) * SUB, :] = jnp.broadcast_to(
                docs[:, h * HD : (h + 1) * HD], (SUB, HD)
            )


def pack(draft_kv, doc_ids):
    rows = doc_ids.shape[0]
    kvl = draft_kv.shape[3] // HD
    depth = 2 * rows + SUB * (rows // HD)
    return pl.pallas_call(
        functools.partial(pack_kernel, kvl, rows),
        grid=(1,),
        out_shape=[
            jax.ShapeDtypeStruct((kvl, depth, HD), BF16),
            jax.ShapeDtypeStruct((1, rows), F32),
        ],
        in_specs=[
            pl.BlockSpec((1, 2, rows, kvl * HD), lambda i: (0, 0, 0, 0)),
            pl.BlockSpec((1, rows), lambda i: (0, 0)),
        ],
        out_specs=[
            pl.BlockSpec((kvl, depth, HD), lambda i: (0, 0, 0)),
            pl.BlockSpec((1, rows), lambda i: (0, 0)),
        ],
        name="pack",
    )(draft_kv, doc_ids.reshape(1, rows))


def stage_kernel(group, rows, steps, sources, first, chained, losses, doc_ref, *refs):
    refs = list(refs)
    last = losses > 0
    pairs = len(sources) // 2
    q_ref = refs.pop(0)
    blocks = [refs.pop(0) for _ in range(2 * pairs)]
    lst_ref = refs.pop(0)
    if first:
        own_ref = refs.pop(0)
    else:
        acc_in = refs.pop(0)
        top_in = refs.pop(0)
    if chained:
        refs = refs[2:]
    loss_refs = [refs.pop(0) for _ in range(losses)]
    if last:
        out_ref, peak_ref, loss_out, acc_out, top_out, q_all, count_ref, flag_ref = refs
    elif first:
        acc_out, top_out, own_s, q_all, count_ref, flag_ref = refs
    else:
        acc_out, top_out, q_all, count_ref, flag_ref = refs
    step = pl.program_id(1)
    opening = (pl.program_id(0) == 0) & (step == 0)
    scale = HD ** (-0.5)
    c2 = scale * LOG2E
    chunks = rows // HD
    lead = lst_ref[...] == 0.0
    for g in range(group):
        q_all[g] = q_ref[0, :, g * HD : (g + 1) * HD]

    @pl.when(opening)
    def _():
        me = lax.axis_index("seq")
        first_doc = doc_ref[0].astype(F32)
        for b, (flip, level) in enumerate(sources):
            source = (me ^ flip) - 4 * level
            below = jnp.zeros((SUB, HD), F32)
            for h in range(chunks):
                docs = blocks[b][0, 2 * rows + h * SUB : 2 * rows + (h + 1) * SUB, :].astype(F32)
                below = below + jnp.where(docs < first_doc, 1.0, 0.0)
            below = (jnp.sum(below) * (1.0 / SUB)).astype(jnp.int32)
            count_ref[b] = jnp.where((source >= 0) & (source < me), below, rows)

    if last:

        @pl.when(opening)
        def _():
            peak = functools.reduce(jnp.maximum, [r[0, 0:1, :] for r in loss_refs])
            total = sum(r[0, 1:2, :] * jnp.exp(r[0, 0:1, :] - peak) for r in loss_refs)
            loss_out[...] = peak + jnp.log(total) - sum(r[0, 2:3, :] for r in loss_refs)

    def values(b):
        parts = [blocks[b][0, rows + h * HD : rows + (h + 1) * HD, :] for h in range(chunks)]
        return jnp.concatenate([jnp.concatenate(parts, axis=1), jnp.ones((SUB, rows), BF16)], axis=0)

    def visit(pair, masked, fresh):
        pick = (2 * pair, 2 * pair + 1)
        vt = jnp.concatenate([values(b) for b in pick], axis=1)
        if masked:
            key_at = lax.broadcasted_iota(jnp.int32, (rows, rows), 0)
            ok = [key_at >= count_ref[b] for b in pick]
            if first:
                tok_at = lax.broadcasted_iota(jnp.int32, (rows, rows), 1)
                ok[0] = (key_at <= tok_at) & (key_at.astype(F32) >= lst_ref[...])
                ok[1] = ok[1] & lead
        waiting = []
        for g in range(group + 2):
            if g < group:
                ref = top_out[0, 0, g : g + 1, :]
                shift = (ref if first else jnp.where(lead, ref, -FILL)) * c2
                best = None
                probs = []
                for i, b in enumerate(pick):
                    s = lax.dot_general(
                        blocks[b][0, 0:rows, :], q_all[g], NT, preferred_element_type=F32
                    )
                    if masked:
                        s = jnp.where(ok[i], s, FILL)
                    m = jnp.max(s.reshape(rows // 8, 8, rows), axis=0)
                    best = m if best is None else jnp.maximum(best, m)
                    probs.append(jnp.exp2(s * c2 - shift).astype(BF16))
                best = jnp.max(best, axis=0, keepdims=True)
                if not first:
                    best = jnp.where(lead, best, FILL)
                top_out[0, 1, g : g + 1, :] = jnp.maximum(top_out[0, 1, g : g + 1, :], best)
                waiting.append((g, jnp.concatenate(probs, axis=0)))
            if g >= 2:
                w, p = waiting.pop(0)
                more = jnp.dot(vt, p, preferred_element_type=F32)[0:KEEP]
                if fresh:
                    acc_out[0, w] = acc_in[0, w] * top_out[0, 2, w : w + 1, :] + more
                else:
                    acc_out[0, w] = acc_out[0, w] + more

    def carry_over():
        for g in range(group):
            acc_out[0, g] = acc_in[0, g] * top_out[0, 2, g : g + 1, :]

    if first:

        ones = jnp.ones((SUB, HD), BF16)

        def diagonal(g, i):
            prod = q_all[g].astype(F32) * own_ref[i, 0].astype(F32)
            high = prod.astype(BF16)
            low = (prod - high.astype(F32)).astype(BF16)
            both = jnp.concatenate([high, low], axis=1)
            wide = jnp.concatenate([ones, ones], axis=1)
            return lax.dot_general(wide, both, NT, preferred_element_type=F32)[0:1]

        for i in range(1, steps):

            @pl.when(step >= i)
            def _():
                for g in range(group):
                    own_s[i, g : g + 1, :] = diagonal(g, i)

            @pl.when(step < i)
            def _():
                own_s[i] = jnp.full((group, rows), FILL, F32)

        for g in range(group):
            near = q_all[g] * own_ref[0, 0]
            own_s[0, g : g + 1, :] = lax.dot_general(ones, near, NT, preferred_element_type=F32)[0:1]
        top_out[0, 1] = functools.reduce(jnp.maximum, [own_s[i] for i in range(1, steps)])
        top_out[0, 0] = jnp.maximum(top_out[0, 1], own_s[0])

        def start():
            weights = [jnp.exp2((own_s[i] - top_out[0, 0]) * c2) for i in range(1, steps)]
            for g in range(group):
                acc_out[0, g, 0:HD] = jnp.zeros((HD, rows), F32)
                acc_out[0, g, HD:KEEP] = jnp.broadcast_to(
                    functools.reduce(jnp.add, weights)[g : g + 1, :], (KEEP - HD, rows)
                )
            for i in range(1, steps):

                @pl.when(step >= i)
                def _():
                    own_val = own_ref[i, 1].astype(F32).T
                    for g in range(group):
                        w = weights[i - 1][g : g + 1, :].astype(BF16).astype(F32)
                        acc_out[0, g, 0:HD] = acc_out[0, g, 0:HD] + own_val * w

    else:
        top_out[0, 0] = top_in[0, 0]
        top_out[0, 1] = top_in[0, 1]
        top_out[0, 2] = jnp.ones((group, rows), F32)

    flag_ref[0] = 1

    @pl.loop(0, 2)
    def _(_):
        @pl.when(flag_ref[0] == 1)
        def _():
            if first:
                start()
                visit(0, True, False)
            else:
                for pair in range(pairs):
                    a, b = count_ref[2 * pair], count_ref[2 * pair + 1]
                    some = jnp.minimum(a, b) < rows
                    full = jnp.maximum(a, b) == 0

                    @pl.when(full)
                    def _():
                        visit(pair, False, pair == 0)

                    @pl.when(some & jnp.logical_not(full))
                    def _():
                        visit(pair, True, pair == 0)

                    if pair == 0:

                        @pl.when(jnp.logical_not(some))
                        def _():
                            carry_over()

            over = jnp.max(top_out[0, 1] - top_out[0, 0]) * c2 > LIMIT
            flag_ref[0] = over.astype(jnp.int32)

            @pl.when(over)
            def _():
                top_out[0, 2] = jnp.exp2((top_out[0, 0] - top_out[0, 1]) * c2)
                top_out[0, 0] = top_out[0, 1]

    if last:
        for g in range(group):
            o = acc_out[0, g, 0:HD] * (1.0 / acc_out[0, g, HD : HD + 1])
            out_ref[0, :, g * HD : (g + 1) * HD] = o.T.astype(BF16)
        peak_ref[0] = top_out[0, 1] * scale


def stage(queries, draft_kv, doc_ids, blocks, lstart, sources, state, losses=(), heads=None):
    steps, rows, width = queries.shape
    kvl = draft_kv.shape[3] // HD
    group = width // HD // kvl
    depth = blocks[0].shape[1]
    first = heads is not None
    low, high = heads if first else (0, kvl)
    chained = first and state is not None
    last = len(losses) > 0
    acc_shape = (kvl * steps, group, KEEP, rows)
    top_shape = (kvl * steps, 3, group, rows)
    acc_spec = pl.BlockSpec((1, group, KEEP, rows), lambda k, j, s: ((k + low) * steps + j, 0, 0, 0))
    top_spec = pl.BlockSpec((1, 3, group, rows), lambda k, j, s: ((k + low) * steps + j, 0, 0, 0))
    row_spec = pl.BlockSpec((1, rows), lambda k, j, s: (0, 0))
    in_specs = (
        [pl.BlockSpec((1, rows, group * HD), lambda k, j, s: (j, 0, k + low))]
        + [pl.BlockSpec((1, depth, HD), lambda k, j, s: (k + low, 0, 0))] * len(blocks)
        + [row_spec]
    )
    args = [queries] + blocks + [lstart]
    scratch = [
        pltpu.VMEM((group, rows, HD), BF16),
        pltpu.SMEM((len(blocks),), jnp.int32),
        pltpu.SMEM((1,), jnp.int32),
    ]
    aliases = {}
    out_shape = [jax.ShapeDtypeStruct(acc_shape, F32), jax.ShapeDtypeStruct(top_shape, F32)]
    out_specs = [acc_spec, top_spec]
    if first:
        args += [draft_kv]
        in_specs += [pl.BlockSpec((steps, 2, rows, HD), lambda k, j, s: (0, 0, 0, k + low))]
        scratch = [pltpu.VMEM((steps, group, rows), F32)] + scratch
    if state is not None:
        aliases = {len(args) + 1: 0, len(args) + 2: 1}
        args += list(state)
        in_specs += [pl.BlockSpec(memory_space=pl.ANY)] * 2 if first else [acc_spec, top_spec]
    if last:
        aliases = {}
        args += losses
        in_specs += [pl.BlockSpec(losses[0].shape, lambda k, j, s: (0, 0, 0))] * len(losses)
        out_shape = [
            jax.ShapeDtypeStruct(queries.shape, BF16),
            jax.ShapeDtypeStruct((steps, kvl * group, rows), F32),
            jax.ShapeDtypeStruct((1, rows), F32),
        ]
        out_specs = [
            pl.BlockSpec((1, rows, group * HD), lambda k, j, s: (j, 0, k)),
            pl.BlockSpec((1, group, rows), lambda k, j, s: (j, k, 0)),
            row_spec,
        ]
        scratch = [
            pltpu.VMEM((1, group, KEEP, rows), F32),
            pltpu.VMEM((1, 3, group, rows), F32),
        ] + scratch
    work = (high - low) * steps * group * rows * rows * len(blocks)
    return pl.pallas_call(
        functools.partial(stage_kernel, group, rows, steps, sources, first, chained, len(losses)),
        out_shape=out_shape,
        grid_spec=pltpu.PrefetchScalarGridSpec(
            num_scalar_prefetch=1,
            grid=(high - low, steps),
            in_specs=in_specs,
            out_specs=out_specs,
            scratch_shapes=scratch,
        ),
        input_output_aliases=aliases,
        name="stage_first" if first else ("stage_last" if last else "stage_mid"),
        compiler_params=pltpu.CompilerParams(vmem_limit_bytes=VMEM),
        cost_estimate=pl.CostEstimate(
            flops=4 * work * HD, transcendentals=work, bytes_accessed=4 * kvl * steps * group * HD * rows
        ),
    )(doc_ids, *args)


def loss_kernel(block, width, tgt_ref, x_ref, out_ref, all_ref):
    i = pl.program_id(0)
    first = i * block
    start_col = lax.axis_index("vocab") * width
    step = min(width, 2048)
    wide = min(width, 512)
    row_at = lax.broadcasted_iota(jnp.int32, (SUB, HD), 0)
    lane_at = lax.broadcasted_iota(jnp.int32, (SUB, HD), 1)

    @pl.loop(0, block // SUB)
    def _(b):
        here = pl.ds(pl.multiple_of(b * SUB, SUB), SUB)
        peak = x_ref[here, 0:step]
        for c in range(1, width // step):
            peak = jnp.maximum(peak, x_ref[here, c * step : (c + 1) * step])
        peak = jnp.max(peak.astype(F32), axis=1, keepdims=True)
        total = jnp.zeros((SUB, wide), F32)
        for c in range(width // wide):
            x = x_ref[here, c * wide : (c + 1) * wide].astype(F32)
            total = total + jnp.exp2((x - peak) * LOG2E)
        total = jnp.sum(total, axis=1, keepdims=True)
        hit = jnp.zeros((SUB, HD), F32)
        for r in range(SUB):
            t = tgt_ref[first + b * SUB + r] - start_col
            inside = (t >= 0) & (t < width)
            lane = jnp.where(inside, t, 0)
            start = pl.multiple_of((lane // HD) * HD, HD)
            x = x_ref[here, pl.ds(start, HD)].astype(F32)
            hit = jnp.where((row_at == r) & (lane_at == lane - start) & inside, x, hit)
        hit = jnp.sum(hit, axis=1, keepdims=True)
        there = pl.ds(pl.multiple_of(first + b * SUB, SUB), SUB)
        all_ref[there, :] = jnp.where(lane_at == 0, peak, jnp.where(lane_at == 1, total, hit))

    @pl.when(i == pl.num_programs(0) - 1)
    def _():
        out_ref[0] = all_ref[...].T[0:8]


def loss_parts(logits, targets):
    rows, width = logits.shape
    block = 64
    return pl.pallas_call(
        functools.partial(loss_kernel, block, width),
        grid_spec=pltpu.PrefetchScalarGridSpec(
            num_scalar_prefetch=1,
            grid=(rows // block,),
            in_specs=[pl.BlockSpec((block, width), lambda i, t: (i, 0))],
            out_specs=pl.BlockSpec((1, 8, rows), lambda i, t: (0, 0, 0)),
            scratch_shapes=[pltpu.VMEM((rows, HD), F32)],
        ),
        out_shape=jax.ShapeDtypeStruct((1, 8, rows), F32),
        name="loss",
        compiler_params=pltpu.CompilerParams(vmem_limit_bytes=VMEM),
        cost_estimate=pl.CostEstimate(
            flops=4 * logits.size, transcendentals=logits.size, bytes_accessed=2 * logits.size
        ),
    )(targets, logits)


def program(queries, draft_kv, doc_ids, logits, targets):
    shards = lax.axis_size("seq")
    halves = lax.axis_size("vocab")
    levels = shards // 4

    def up(x):
        return lax.ppermute(x, "seq", [(i, i + 4) for i in range(shards - 4)])

    def swap(x, bit):
        return lax.ppermute(x, "seq", [(i, i ^ bit) for i in range(shards)])

    mine, lstart = pack(draft_kv, doc_ids)
    z, x, c, d = [mine], [], [], []

    def spread(level):
        if level + 1 < levels:
            z.append(up(z[level]))
        c.append(swap(z[level], 1))
        x.append(swap(z[level], 2))
        if level > 0:
            d.append(swap(x[level - 1], 1))
        if level + 1 == levels:
            d.append(swap(z[level], 3))

    spread(0)
    parts = loss_parts(logits, targets)
    z[1], x[0], parts = lax.optimization_barrier((z[1], x[0], parts))
    spread(1)
    losses = [parts] + [
        lax.ppermute(parts, "vocab", [(i, (i + t) % halves) for i in range(halves)])
        for t in range(1, halves)
    ]

    def run(picked, state, **more):
        names = {"z": (z, 0), "c": (c, 1), "x": (x, 2), "d": (d, 3)}
        blocks = [names[name][0][level] for name, level in picked]
        sources = [(names[name][1], level) for name, level in picked]
        return stage(queries, draft_kv, doc_ids, blocks, lstart, sources, state, **more)

    kvl = draft_kv.shape[3] // HD
    cuts = [0, kvl // 2, kvl] if kvl > 1 else [0, kvl]
    state = None
    for low, high in zip(cuts, cuts[1:]):
        state = run([("z", 0), ("c", 0)], state, heads=(low, high))
        level = len(c)
        if level < levels:
            z[level], x[level - 1], top = lax.optimization_barrier((z[level], x[level - 1], state[1]))
            state = [state[0], top]
            spread(level)
    while len(c) < levels:
        spread(len(c))
    rest = [("x", 0), ("d", 0)]
    for level in range(1, levels):
        rest += [(name, level) for name in "zcxd"]
    split = [0, 6] + list(range(14, len(rest) + 1, 8))
    for begin, end in zip(split, split[1:]):
        final = end == len(rest)
        state = run(rest[begin:end], state, losses=losses if final else [])
    out, peaks, token_loss = state
    return (out, peaks.transpose(0, 2, 1), token_loss.reshape(-1))


def solution(mesh):
    in_specs = (
        P(None, "seq", "vocab"),
        P(None, None, "seq", "vocab"),
        P("seq"),
        P("seq", "vocab"),
        P("seq"),
    )
    out_specs = (P(None, "seq", "vocab"), P(None, "seq", "vocab"), P("seq"))
    return jax.shard_map(program, mesh=mesh, in_specs=in_specs, out_specs=out_specs, check_vma=False)
```

```python
import functools

import jax
import jax.numpy as jnp
from jax import lax
from jax.experimental import pallas as pl
from jax.experimental.pallas import tpu as pltpu
from jax.sharding import PartitionSpec as P


HD = 128
SUB = 16
LOG2E = 1.4426950408889634
FILL = -1e30
NT = (((1,), (1,)), ((), ()))
LIMIT = 60.0
KEEP = HD + 8
VMEM = 67043328
F32 = jnp.float32
BF16 = jnp.bfloat16


def pack_kernel(kvl, rows, kv_ref, doc_ref, out_ref, lst_ref):
    chunks = rows // HD
    along = jnp.broadcast_to(doc_ref[...].astype(F32), (rows, rows))
    lst_ref[...] = jnp.sum(jnp.where(along.T < along, 1.0, 0.0), axis=0, keepdims=True)
    for k in range(kvl):
        cols = slice(k * HD, (k + 1) * HD)
        out_ref[k, 0:rows, :] = kv_ref[0, 0, :, cols]
        vt = kv_ref[0, 1, :, cols].astype(F32).T.astype(BF16)
        docs = doc_ref[...].astype(F32).astype(BF16)
        for h in range(chunks):
            out_ref[k, rows + h * HD : rows + (h + 1) * HD, :] = vt[:, h * HD : (h + 1) * HD]
            out_ref[k, 2 * rows + h * SUB : 2 * rows + (h + 1) * SUB, :] = jnp.broadcast_to(
                docs[:, h * HD : (h + 1) * HD], (SUB, HD)
            )


def pack(draft_kv, doc_ids):
    rows = doc_ids.shape[0]
    kvl = draft_kv.shape[3] // HD
    depth = 2 * rows + SUB * (rows // HD)
    return pl.pallas_call(
        functools.partial(pack_kernel, kvl, rows),
        grid=(1,),
        out_shape=[
            jax.ShapeDtypeStruct((kvl, depth, HD), BF16),
            jax.ShapeDtypeStruct((1, rows), F32),
        ],
        in_specs=[
            pl.BlockSpec((1, 2, rows, kvl * HD), lambda i: (0, 0, 0, 0)),
            pl.BlockSpec((1, rows), lambda i: (0, 0)),
        ],
        out_specs=[
            pl.BlockSpec((kvl, depth, HD), lambda i: (0, 0, 0)),
            pl.BlockSpec((1, rows), lambda i: (0, 0)),
        ],
        name="pack",
    )(draft_kv, doc_ids.reshape(1, rows))


def stage_kernel(group, rows, steps, sources, first, chained, losses, doc_ref, *refs):
    refs = list(refs)
    last = losses > 0
    pairs = len(sources) // 2
    q_ref = refs.pop(0)
    blocks = [refs.pop(0) for _ in range(2 * pairs)]
    lst_ref = refs.pop(0)
    if first:
        own_ref = refs.pop(0)
    else:
        acc_in = refs.pop(0)
        top_in = refs.pop(0)
    if chained:
        refs = refs[2:]
    loss_refs = [refs.pop(0) for _ in range(losses)]
    if last:
        out_ref, peak_ref, loss_out, acc_out, top_out, q_all, count_ref = refs
    elif first:
        acc_out, top_out, own_s, bias_ref, q_all, count_ref = refs
    else:
        acc_out, top_out, q_all, count_ref = refs
    step = pl.program_id(1)
    opening = (pl.program_id(0) == 0) & (step == 0)
    scale = HD ** (-0.5)
    c2 = scale * LOG2E
    chunks = rows // HD
    lead = lst_ref[...] == 0.0
    for g in range(group):
        q_all[g] = q_ref[0, :, g * HD : (g + 1) * HD]

    @pl.when(opening)
    def _():
        me = lax.axis_index("seq")
        first_doc = doc_ref[0].astype(F32)
        for b, (flip, level) in enumerate(sources):
            source = (me ^ flip) - 4 * level
            below = jnp.zeros((SUB, HD), F32)
            for h in range(chunks):
                docs = blocks[b][0, 2 * rows + h * SUB : 2 * rows + (h + 1) * SUB, :].astype(F32)
                below = below + jnp.where(docs < first_doc, 1.0, 0.0)
            below = (jnp.sum(below) * (1.0 / SUB)).astype(jnp.int32)
            count_ref[b] = jnp.where((source >= 0) & (source < me), below, rows)

    if last:

        @pl.when(opening)
        def _():
            peak = functools.reduce(jnp.maximum, [r[0, 0:1, :] for r in loss_refs])
            total = sum(r[0, 1:2, :] * jnp.exp(r[0, 0:1, :] - peak) for r in loss_refs)
            loss_out[...] = peak + jnp.log(total) - sum(r[0, 2:3, :] for r in loss_refs)

    def values(b):
        parts = [blocks[b][0, rows + h * HD : rows + (h + 1) * HD, :] for h in range(chunks)]
        return jnp.concatenate(parts, axis=1)

    def folded(v, op):
        return op(v.reshape(rows // 8, 8, rows), axis=0)

    def usable(pair):
        key_at = lax.broadcasted_iota(jnp.int32, (rows, rows), 0)
        ok = [key_at >= count_ref[2 * pair + i] for i in range(2)]
        if first:
            tok_at = lax.broadcasted_iota(jnp.int32, (rows, rows), 1)
            ok[0] = (key_at <= tok_at) & (key_at.astype(F32) >= lst_ref[...])
            ok[1] = ok[1] & lead
        return ok

    def scores(pair, i, q):
        return lax.dot_general(
            blocks[2 * pair + i][0, 0:rows, :], q, NT, preferred_element_type=F32
        )

    def pair_values(pair):
        return jnp.concatenate([values(2 * pair), values(2 * pair + 1)], axis=1)

    def visit(chosen, masked, fresh):
        units = [(g, pair) for g in range(group) for pair in chosen]
        vts = {pair: pair_values(pair) for pair in chosen}
        oks = {pair: usable(pair) for pair in chosen} if masked and not first else {}
        best, sums = {}, {}
        waiting = []
        for n in range(len(units) + 2):
            if n < len(units):
                g, pair = units[n]
                probs = []
                for i in range(2):
                    s = scores(pair, i, q_all[g])
                    if first:
                        s = s + bias_ref[i]
                    elif masked:
                        s = jnp.where(oks[pair][i], s, FILL)
                    m = folded(s, jnp.max)
                    best[g] = jnp.maximum(best[g], m) if g in best else m
                    p = jnp.exp2(s * c2)
                    t = folded(p, jnp.sum)
                    sums[g] = sums[g] + t if g in sums else t
                    probs.append(p.astype(BF16))
                if pair == chosen[-1]:
                    peak = jnp.max(best.pop(g), axis=0, keepdims=True)
                    if not first:
                        peak = jnp.where(lead, peak, FILL)
                    top_out[0, 1, g : g + 1, :] = jnp.maximum(top_out[0, 1, g : g + 1, :], peak)
                waiting.append((g, pair, jnp.concatenate(probs, axis=0)))
            if n >= 2:
                g, pair, p = waiting.pop(0)
                more = jnp.dot(vts[pair], p, preferred_element_type=F32)
                old = acc_in if fresh and pair == chosen[0] else acc_out
                acc_out[0, g, 0:HD] = old[0, g, 0:HD] + (more if first else jnp.where(lead, more, 0.0))
                if pair == chosen[-1]:
                    more = sums.pop(g)
                    old = acc_in if fresh else acc_out
                    acc_out[0, g, HD:KEEP] = old[0, g, HD:KEEP] + (
                        more if first else jnp.where(lead, more, 0.0)
                    )

    def revisit(pair):
        ok = usable(pair)
        if not first:
            ok = [one & lead for one in ok]
        vt = pair_values(pair)

        @pl.loop(0, group)
        def _(g):
            shift = top_out[0, 0, pl.ds(g, 1), :] * c2
            probs = [
                jnp.exp2(jnp.where(ok[i], scores(pair, i, q_all[g]), FILL) * c2 - shift) for i in range(2)
            ]
            acc_out[0, g, HD:KEEP] = acc_out[0, g, HD:KEEP] + sum(folded(p, jnp.sum) for p in probs)
            p = jnp.concatenate(probs, axis=0).astype(BF16)
            acc_out[0, g, 0:HD] = acc_out[0, g, 0:HD] + jnp.dot(vt, p, preferred_element_type=F32)

    if first:

        @pl.when(opening)
        def _():
            for i, ok in enumerate(usable(0)):
                bias_ref[i] = jnp.where(ok, 0.0, FILL)


        ones = jnp.ones((SUB, HD), BF16)

        def diagonal(g, i):
            prod = q_all[g].astype(F32) * own_ref[i, 0].astype(F32)
            high = prod.astype(BF16)
            low = (prod - high.astype(F32)).astype(BF16)
            both = jnp.concatenate([high, low], axis=1)
            wide = jnp.concatenate([ones, ones], axis=1)
            return lax.dot_general(wide, both, NT, preferred_element_type=F32)[0:1]

        for i in range(1, steps):

            @pl.when(step >= i)
            def _():
                for g in range(group):
                    own_s[i, g : g + 1, :] = diagonal(g, i)

            @pl.when(step < i)
            def _():
                own_s[i] = jnp.full((group, rows), FILL, F32)

        top_out[0, 0] = jnp.zeros((group, rows), F32)
        top_out[0, 1] = functools.reduce(jnp.maximum, [own_s[i] for i in range(1, steps)])

        def start():
            weights = [jnp.exp2((own_s[i] - top_out[0, 0]) * c2) for i in range(1, steps)]
            for g in range(group):
                acc_out[0, g, 0:HD] = jnp.zeros((HD, rows), F32)
                acc_out[0, g, HD:KEEP] = jnp.broadcast_to(
                    functools.reduce(jnp.add, weights)[g : g + 1, :] * (1.0 / (KEEP - HD)), (KEEP - HD, rows)
                )
            for i in range(1, steps):

                @pl.when(step >= i)
                def _():
                    own_val = own_ref[i, 1].astype(F32).T
                    for g in range(group):
                        w = weights[i - 1][g : g + 1, :].astype(BF16).astype(F32)
                        acc_out[0, g, 0:HD] = acc_out[0, g, 0:HD] + own_val * w

        start()
        visit([0], True, False)
        spread = jnp.max(jnp.abs(top_out[0, 1])) * c2

        @pl.when(spread > LIMIT)
        def _():
            top_out[0, 0] = top_out[0, 1]
            start()
            revisit(0)

    else:
        top_out[...] = top_in[...]
        some, full = [], []
        for pair in range(pairs):
            a, b = count_ref[2 * pair], count_ref[2 * pair + 1]
            some.append(jnp.minimum(a, b) < rows)
            full.append(jnp.maximum(a, b) == 0)
        joined = list(range(2 if last else pairs))
        all_full = functools.reduce(jnp.logical_and, [full[pair] for pair in joined])

        @pl.when(all_full)
        def _():
            visit(joined, False, True)

        @pl.when(jnp.logical_not(all_full))
        def _():
            for g in range(group):
                acc_out[0, g] = acc_in[0, g]

        for pair in range(pairs):

            @pl.when(some[pair] & jnp.logical_not(all_full & (pair in joined)))
            def _():
                visit([pair], True, False)

        past = top_in[0, 0]
        spread = jnp.maximum(jnp.max(top_out[0, 1]) * c2 - LIMIT, jnp.max(jnp.abs(past)))

        @pl.when(spread > 0.0)
        def _():
            top_out[0, 0] = top_out[0, 1]
            fade = jnp.exp2((past - top_out[0, 1]) * c2)
            for g in range(group):
                acc_out[0, g] = acc_in[0, g] * fade[g : g + 1, :]
            for pair in range(pairs):

                @pl.when(some[pair])
                def _():
                    revisit(pair)

    if last:
        for g in range(group):
            o = acc_out[0, g, 0:HD] * (1.0 / jnp.sum(acc_out[0, g, HD:KEEP], axis=0, keepdims=True))
            out_ref[0, :, g * HD : (g + 1) * HD] = o.T.astype(BF16)
        peak_ref[0] = top_out[0, 1] * scale


def stage(queries, draft_kv, doc_ids, blocks, lstart, sources, state, losses=(), heads=None):
    steps, rows, width = queries.shape
    kvl = draft_kv.shape[3] // HD
    group = width // HD // kvl
    depth = blocks[0].shape[1]
    first = heads is not None
    low, high = heads if first else (0, kvl)
    chained = first and state is not None
    last = len(losses) > 0
    acc_shape = (kvl * steps, group, KEEP, rows)
    top_shape = (kvl * steps, 2, group, rows)
    acc_spec = pl.BlockSpec((1, group, KEEP, rows), lambda k, j, s: ((k + low) * steps + j, 0, 0, 0))
    top_spec = pl.BlockSpec((1, 2, group, rows), lambda k, j, s: ((k + low) * steps + j, 0, 0, 0))
    row_spec = pl.BlockSpec((1, rows), lambda k, j, s: (0, 0))
    in_specs = (
        [pl.BlockSpec((1, rows, group * HD), lambda k, j, s: (j, 0, k + low))]
        + [pl.BlockSpec((1, depth, HD), lambda k, j, s: (k + low, 0, 0))] * len(blocks)
        + [row_spec]
    )
    args = [queries] + blocks + [lstart]
    scratch = [
        pltpu.VMEM((group, rows, HD), BF16),
        pltpu.SMEM((len(blocks),), jnp.int32),
    ]
    aliases = {}
    out_shape = [jax.ShapeDtypeStruct(acc_shape, F32), jax.ShapeDtypeStruct(top_shape, F32)]
    out_specs = [acc_spec, top_spec]
    if first:
        args += [draft_kv]
        in_specs += [pl.BlockSpec((steps, 2, rows, HD), lambda k, j, s: (0, 0, 0, k + low))]
        scratch = [
            pltpu.VMEM((steps, group, rows), F32),
            pltpu.VMEM((2, rows, rows), F32),
        ] + scratch
    if state is not None:
        aliases = {len(args) + 1: 0, len(args) + 2: 1}
        args += list(state)
        in_specs += [pl.BlockSpec(memory_space=pl.ANY)] * 2 if first else [acc_spec, top_spec]
    if last:
        aliases = {}
        args += losses
        in_specs += [pl.BlockSpec(losses[0].shape, lambda k, j, s: (0, 0, 0))] * len(losses)
        out_shape = [
            jax.ShapeDtypeStruct(queries.shape, BF16),
            jax.ShapeDtypeStruct((steps, kvl * group, rows), F32),
            jax.ShapeDtypeStruct((1, rows), F32),
        ]
        out_specs = [
            pl.BlockSpec((1, rows, group * HD), lambda k, j, s: (j, 0, k)),
            pl.BlockSpec((1, group, rows), lambda k, j, s: (j, k, 0)),
            row_spec,
        ]
        scratch = [
            pltpu.VMEM((1, group, KEEP, rows), F32),
            pltpu.VMEM((1, 2, group, rows), F32),
        ] + scratch
    work = (high - low) * steps * group * rows * rows * len(blocks)
    return pl.pallas_call(
        functools.partial(stage_kernel, group, rows, steps, sources, first, chained, len(losses)),
        out_shape=out_shape,
        grid_spec=pltpu.PrefetchScalarGridSpec(
            num_scalar_prefetch=1,
            grid=(high - low, steps),
            in_specs=in_specs,
            out_specs=out_specs,
            scratch_shapes=scratch,
        ),
        input_output_aliases=aliases,
        name="stage_first" if first else ("stage_last" if last else "stage_mid"),
        compiler_params=pltpu.CompilerParams(vmem_limit_bytes=VMEM),
        cost_estimate=pl.CostEstimate(
            flops=4 * work * HD, transcendentals=work, bytes_accessed=4 * kvl * steps * group * HD * rows
        ),
    )(doc_ids, *args)


def loss_kernel(block, width, tgt_ref, x_ref, out_ref, all_ref):
    i = pl.program_id(0)
    first = i * block
    start_col = lax.axis_index("vocab") * width
    step = min(width, 2048)
    wide = min(width, 512)
    row_at = lax.broadcasted_iota(jnp.int32, (SUB, HD), 0)
    lane_at = lax.broadcasted_iota(jnp.int32, (SUB, HD), 1)

    @pl.loop(0, block // SUB)
    def _(b):
        here = pl.ds(pl.multiple_of(b * SUB, SUB), SUB)
        peak = x_ref[here, 0:step]
        for c in range(1, width // step):
            peak = jnp.maximum(peak, x_ref[here, c * step : (c + 1) * step])
        peak = jnp.max(peak.astype(F32), axis=1, keepdims=True)
        total = jnp.zeros((SUB, wide), F32)
        for c in range(width // wide):
            x = x_ref[here, c * wide : (c + 1) * wide].astype(F32)
            total = total + jnp.exp2((x - peak) * LOG2E)
        total = jnp.sum(total, axis=1, keepdims=True)
        hit = jnp.zeros((SUB, HD), F32)
        for r in range(SUB):
            t = tgt_ref[first + b * SUB + r] - start_col
            inside = (t >= 0) & (t < width)
            lane = jnp.where(inside, t, 0)
            start = pl.multiple_of((lane // HD) * HD, HD)
            x = x_ref[here, pl.ds(start, HD)].astype(F32)
            hit = jnp.where((row_at == r) & (lane_at == lane - start) & inside, x, hit)
        hit = jnp.sum(hit, axis=1, keepdims=True)
        there = pl.ds(pl.multiple_of(first + b * SUB, SUB), SUB)
        all_ref[there, :] = jnp.where(lane_at == 0, peak, jnp.where(lane_at == 1, total, hit))

    @pl.when(i == pl.num_programs(0) - 1)
    def _():
        out_ref[0] = all_ref[...].T[0:8]


def loss_parts(logits, targets):
    rows, width = logits.shape
    block = 64
    return pl.pallas_call(
        functools.partial(loss_kernel, block, width),
        grid_spec=pltpu.PrefetchScalarGridSpec(
            num_scalar_prefetch=1,
            grid=(rows // block,),
            in_specs=[pl.BlockSpec((block, width), lambda i, t: (i, 0))],
            out_specs=pl.BlockSpec((1, 8, rows), lambda i, t: (0, 0, 0)),
            scratch_shapes=[pltpu.VMEM((rows, HD), F32)],
        ),
        out_shape=jax.ShapeDtypeStruct((1, 8, rows), F32),
        name="loss",
        compiler_params=pltpu.CompilerParams(vmem_limit_bytes=VMEM),
        cost_estimate=pl.CostEstimate(
            flops=4 * logits.size, transcendentals=logits.size, bytes_accessed=2 * logits.size
        ),
    )(targets, logits)


def program(queries, draft_kv, doc_ids, logits, targets):
    shards = lax.axis_size("seq")
    halves = lax.axis_size("vocab")
    levels = shards // 4

    def up(x):
        return lax.ppermute(x, "seq", [(i, i + 4) for i in range(shards - 4)])

    def swap(x, bit):
        return lax.ppermute(x, "seq", [(i, i ^ bit) for i in range(shards)])

    mine, lstart = pack(draft_kv, doc_ids)
    z, x, c, d = [mine], [], [], []

    def spread(level):
        if level + 1 < levels:
            z.append(up(z[level]))
        c.append(swap(z[level], 1))
        x.append(swap(z[level], 2))
        if level > 0:
            d.append(swap(x[level - 1], 1))
        if level + 1 == levels:
            d.append(swap(z[level], 3))

    spread(0)
    parts = loss_parts(logits, targets)
    z[1], x[0], parts = lax.optimization_barrier((z[1], x[0], parts))
    spread(1)
    losses = [parts] + [
        lax.ppermute(parts, "vocab", [(i, (i + t) % halves) for i in range(halves)])
        for t in range(1, halves)
    ]

    def run(picked, state, **more):
        names = {"z": (z, 0), "c": (c, 1), "x": (x, 2), "d": (d, 3)}
        blocks = [names[name][0][level] for name, level in picked]
        sources = [(names[name][1], level) for name, level in picked]
        return stage(queries, draft_kv, doc_ids, blocks, lstart, sources, state, **more)

    kvl = draft_kv.shape[3] // HD
    cuts = [0, kvl // 2, kvl] if kvl > 1 else [0, kvl]
    state = None
    for low, high in zip(cuts, cuts[1:]):
        state = run([("z", 0), ("c", 0)], state, heads=(low, high))
        level = len(c)
        if level < levels:
            z[level], x[level - 1], top = lax.optimization_barrier((z[level], x[level - 1], state[1]))
            state = [state[0], top]
            spread(level)
    while len(c) < levels:
        spread(len(c))
    rest = [("x", 0), ("d", 0)]
    for level in range(1, levels):
        rest += [(name, level) for name in "zcxd"]
    split = [0, 6] + list(range(14, len(rest) + 1, 8))
    for begin, end in zip(split, split[1:]):
        final = end == len(rest)
        state = run(rest[begin:end], state, losses=losses if final else [])
    out, peaks, token_loss = state
    return (out, peaks.transpose(0, 2, 1), token_loss.reshape(-1))


def solution(mesh):
    in_specs = (
        P(None, "seq", "vocab"),
        P(None, None, "seq", "vocab"),
        P("seq"),
        P("seq", "vocab"),
        P("seq"),
    )
    out_specs = (P(None, "seq", "vocab"), P(None, "seq", "vocab"), P("seq"))
    return jax.shard_map(program, mesh=mesh, in_specs=in_specs, out_specs=out_specs, check_vma=False)
```

```python
import functools

import jax
import jax.numpy as jnp
from jax import lax
from jax.experimental import pallas as pl
from jax.experimental.pallas import tpu as pltpu
from jax.sharding import PartitionSpec as P


HD = 128
SUB = 16
LOG2E = 1.4426950408889634
FILL = -1e30
NT = (((1,), (1,)), ((), ()))
LIMIT = 60.0
KEEP = HD + 8
VMEM = 67043328
F32 = jnp.float32
BF16 = jnp.bfloat16


def pack_kernel(kvl, rows, kv_ref, doc_ref, out_ref, lst_ref):
    chunks = rows // HD
    along = jnp.broadcast_to(doc_ref[...].astype(F32), (rows, rows))
    lst_ref[...] = jnp.sum(jnp.where(along.T < along, 1.0, 0.0), axis=0, keepdims=True)
    for k in range(kvl):
        cols = slice(k * HD, (k + 1) * HD)
        out_ref[k, 0:rows, :] = kv_ref[0, 0, :, cols]
        vt = kv_ref[0, 1, :, cols].astype(F32).T.astype(BF16)
        docs = doc_ref[...].astype(F32).astype(BF16)
        for h in range(chunks):
            out_ref[k, rows + h * HD : rows + (h + 1) * HD, :] = vt[:, h * HD : (h + 1) * HD]
            out_ref[k, 2 * rows + h * SUB : 2 * rows + (h + 1) * SUB, :] = jnp.broadcast_to(
                docs[:, h * HD : (h + 1) * HD], (SUB, HD)
            )


def pack(draft_kv, doc_ids):
    rows = doc_ids.shape[0]
    kvl = draft_kv.shape[3] // HD
    depth = 2 * rows + SUB * (rows // HD)
    return pl.pallas_call(
        functools.partial(pack_kernel, kvl, rows),
        grid=(1,),
        out_shape=[
            jax.ShapeDtypeStruct((kvl, depth, HD), BF16),
            jax.ShapeDtypeStruct((1, rows), F32),
        ],
        in_specs=[
            pl.BlockSpec((1, 2, rows, kvl * HD), lambda i: (0, 0, 0, 0)),
            pl.BlockSpec((1, rows), lambda i: (0, 0)),
        ],
        out_specs=[
            pl.BlockSpec((kvl, depth, HD), lambda i: (0, 0, 0)),
            pl.BlockSpec((1, rows), lambda i: (0, 0)),
        ],
        name="pack",
    )(draft_kv, doc_ids.reshape(1, rows))


def stage_kernel(group, rows, steps, sources, first, chained, losses, doc_ref, *refs):
    refs = list(refs)
    last = losses > 0
    pairs = len(sources) // 2
    q_ref = refs.pop(0)
    q_all = q_ref
    blocks = [refs.pop(0) for _ in range(2 * pairs)]
    lst_ref = refs.pop(0)
    if first:
        own_ref = refs.pop(0)
    else:
        acc_in = refs.pop(0)
        top_in = refs.pop(0)
    if chained:
        refs = refs[3:]
    loss_refs = [refs.pop(0) for _ in range(losses)]
    if last:
        out_ref, peak_ref, loss_out, acc_out, top_out, count_ref = refs
    elif first:
        acc_out, top_out, q_all, own_s, bias_ref, count_ref = refs
    else:
        acc_out, top_out, count_ref = refs
    step = pl.program_id(1)
    opening = (pl.program_id(0) == 0) & (step == 0)
    scale = HD ** (-0.5)
    c2 = scale * LOG2E
    chunks = rows // HD
    lead = lst_ref[...] == 0.0
    if first:
        for g in range(group):
            q_all[0, g] = q_ref[0, :, g * HD : (g + 1) * HD]

    @pl.when(opening)
    def _():
        me = lax.axis_index("seq")
        first_doc = doc_ref[0].astype(F32)
        for b, (flip, level) in enumerate(sources):
            source = (me ^ flip) - 4 * level
            below = jnp.zeros((SUB, HD), F32)
            for h in range(chunks):
                docs = blocks[b][0, 2 * rows + h * SUB : 2 * rows + (h + 1) * SUB, :].astype(F32)
                below = below + jnp.where(docs < first_doc, 1.0, 0.0)
            below = (jnp.sum(below) * (1.0 / SUB)).astype(jnp.int32)
            count_ref[b] = jnp.where((source >= 0) & (source < me), below, rows)

    if last:

        @pl.when(opening)
        def _():
            peak = functools.reduce(jnp.maximum, [r[0, 0:1, :] for r in loss_refs])
            total = sum(r[0, 1:2, :] * jnp.exp(r[0, 0:1, :] - peak) for r in loss_refs)
            loss_out[...] = peak + jnp.log(total) - sum(r[0, 2:3, :] for r in loss_refs)

    def values(b):
        parts = [blocks[b][0, rows + h * HD : rows + (h + 1) * HD, :] for h in range(chunks)]
        return jnp.concatenate([jnp.concatenate(parts, axis=1), jnp.ones((SUB, rows), BF16)], axis=0)

    def folded(v, op):
        return op(v.reshape(rows // 8, 8, rows), axis=0)

    def usable(pair):
        key_at = lax.broadcasted_iota(jnp.int32, (rows, rows), 0)
        ok = [key_at >= count_ref[2 * pair + i] for i in range(2)]
        if first:
            tok_at = lax.broadcasted_iota(jnp.int32, (rows, rows), 1)
            ok[0] = (key_at <= tok_at) & (key_at.astype(F32) >= lst_ref[...])
            ok[1] = ok[1] & lead
        return ok

    def scores(pair, i, q):
        return lax.dot_general(
            blocks[2 * pair + i][0, 0:rows, :], q, NT, preferred_element_type=F32
        )

    def pair_values(pair, count=2):
        return jnp.concatenate([values(2 * pair + i) for i in range(count)], axis=1)

    def visit(chosen, masked, fresh, count=2):
        units = [(g, pair) for g in range(group) for pair in chosen]
        vts = {pair: pair_values(pair, count) for pair in chosen}
        oks = {pair: usable(pair) for pair in chosen} if masked and not first else {}
        best = {}
        waiting = []
        late = 4 // count
        for n in range(len(units) + late):
            if n < len(units):
                g, pair = units[n]
                probs = []
                for i in range(count):
                    s = scores(pair, i, q_all[0, g])
                    if first:
                        s = s + bias_ref[i]
                    elif masked:
                        s = jnp.where(oks[pair][i], s, FILL)
                    m = folded(s, jnp.max)
                    best[g] = jnp.maximum(best[g], m) if g in best else m
                    probs.append(jnp.exp2(s * c2).astype(BF16))
                if pair == chosen[-1]:
                    peak = jnp.max(best.pop(g), axis=0, keepdims=True)
                    if not first:
                        peak = jnp.where(lead, peak, FILL)
                    top_out[0, 1, g : g + 1, :] = jnp.maximum(top_out[0, 1, g : g + 1, :], peak)
                waiting.append((g, pair, jnp.concatenate(probs, axis=0)))
            if n >= late:
                g, pair, p = waiting.pop(0)
                more = jnp.dot(vts[pair], p, preferred_element_type=F32)[0:KEEP]
                old = acc_in if fresh and pair == chosen[0] else acc_out
                acc_out[0, g] = old[0, g] + (more if first else jnp.where(lead, more, 0.0))

    def revisit(pair):
        ok = usable(pair)
        if not first:
            ok = [one & lead for one in ok]
        vt = pair_values(pair)

        @pl.loop(0, group)
        def _(g):
            shift = top_out[0, 0, pl.ds(g, 1), :] * c2
            probs = [
                jnp.exp2(jnp.where(ok[i], scores(pair, i, q_all[0, g]), FILL) * c2 - shift) for i in range(2)
            ]
            p = jnp.concatenate(probs, axis=0).astype(BF16)
            acc_out[0, g] = acc_out[0, g] + jnp.dot(vt, p, preferred_element_type=F32)[0:KEEP]

    if first:

        @pl.when(opening)
        def _():
            for i, ok in enumerate(usable(0)):
                bias_ref[i] = jnp.where(ok, 0.0, FILL)


        ones = jnp.ones((SUB, HD), BF16)

        def diagonal(g, i):
            prod = q_all[0, g].astype(F32) * own_ref[i, 0].astype(F32)
            high = prod.astype(BF16)
            low = (prod - high.astype(F32)).astype(BF16)
            both = jnp.concatenate([high, low], axis=1)
            wide = jnp.concatenate([ones, ones], axis=1)
            return lax.dot_general(wide, both, NT, preferred_element_type=F32)[0:1]

        for i in range(1, steps):

            @pl.when(step >= i)
            def _():
                for g in range(group):
                    own_s[i, g : g + 1, :] = diagonal(g, i)

            @pl.when(step < i)
            def _():
                own_s[i] = jnp.full((group, rows), FILL, F32)

        top_out[0, 0] = jnp.zeros((group, rows), F32)
        top_out[0, 1] = functools.reduce(jnp.maximum, [own_s[i] for i in range(1, steps)])

        def start():
            weights = [jnp.exp2((own_s[i] - top_out[0, 0]) * c2) for i in range(1, steps)]
            for g in range(group):
                acc_out[0, g, 0:HD] = jnp.zeros((HD, rows), F32)
                acc_out[0, g, HD:KEEP] = jnp.broadcast_to(
                    functools.reduce(jnp.add, weights)[g : g + 1, :], (KEEP - HD, rows)
                )
            for i in range(1, steps):

                @pl.when(step >= i)
                def _():
                    own_val = own_ref[i, 1].astype(F32).T
                    for g in range(group):
                        w = weights[i - 1][g : g + 1, :].astype(BF16).astype(F32)
                        acc_out[0, g, 0:HD] = acc_out[0, g, 0:HD] + own_val * w

        start()

        @pl.when(count_ref[1] < rows)
        def _():
            visit([0], True, False)

        @pl.when(count_ref[1] >= rows)
        def _():
            visit([0], True, False, 1)

        spread = jnp.max(jnp.abs(top_out[0, 1])) * c2

        @pl.when(spread > LIMIT)
        def _():
            top_out[0, 0] = top_out[0, 1]
            start()
            revisit(0)

    else:
        top_out[...] = top_in[...]
        some, full = [], []
        for pair in range(pairs):
            a, b = count_ref[2 * pair], count_ref[2 * pair + 1]
            some.append(jnp.minimum(a, b) < rows)
            full.append(jnp.maximum(a, b) == 0)
        joined = list(range(2 if last else pairs))
        all_full = functools.reduce(jnp.logical_and, [full[pair] for pair in joined])

        @pl.when(all_full)
        def _():
            visit(joined, False, True)

        @pl.when(jnp.logical_not(all_full))
        def _():
            for g in range(group):
                acc_out[0, g] = acc_in[0, g]

        for pair in range(pairs):

            alone = some[pair] & jnp.logical_not(all_full & (pair in joined))
            plain = full[pair] if last and pair not in joined else False

            half = (count_ref[2 * pair + 1] >= rows) if last else False

            @pl.when(alone & jnp.logical_not(plain) & jnp.logical_not(half))
            def _():
                visit([pair], True, False)

            if last:

                @pl.when(alone & half)
                def _():
                    visit([pair], True, False, 1)

            if last and pair not in joined:

                @pl.when(alone & plain)
                def _():
                    visit([pair], False, False)

        past = top_in[0, 0]
        spread = jnp.maximum(jnp.max(top_out[0, 1]) * c2 - LIMIT, jnp.max(jnp.abs(past)))

        @pl.when(spread > 0.0)
        def _():
            top_out[0, 0] = top_out[0, 1]
            fade = jnp.exp2((past - top_out[0, 1]) * c2)
            for g in range(group):
                acc_out[0, g] = acc_in[0, g] * fade[g : g + 1, :]
            for pair in range(pairs):

                @pl.when(some[pair])
                def _():
                    revisit(pair)

    if last:
        for g in range(group):
            o = acc_out[0, g, 0:HD] * (1.0 / acc_out[0, g, HD : HD + 1])
            out_ref[0, :, g * HD : (g + 1) * HD] = o.astype(BF16).T
        peak_ref[0] = top_out[0, 1] * scale


def stage(queries, draft_kv, doc_ids, blocks, lstart, sources, state, losses=(), heads=None):
    steps, rows, width = queries.shape
    kvl = draft_kv.shape[3] // HD
    group = width // HD // kvl
    depth = blocks[0].shape[1]
    first = heads is not None
    low, high = heads if first else (0, kvl)
    chained = first and state is not None
    last = len(losses) > 0
    acc_shape = (kvl * steps, group, KEEP, rows)
    top_shape = (kvl * steps, 2, group, rows)
    acc_spec = pl.BlockSpec((1, group, KEEP, rows), lambda k, j, s: ((k + low) * steps + j, 0, 0, 0))
    top_spec = pl.BlockSpec((1, 2, group, rows), lambda k, j, s: ((k + low) * steps + j, 0, 0, 0))
    row_spec = pl.BlockSpec((1, rows), lambda k, j, s: (0, 0))
    wide_spec = pl.BlockSpec((1, rows, group * HD), lambda k, j, s: (j, 0, k + low))
    tile_spec = pl.BlockSpec((1, group, rows, HD), lambda k, j, s: ((k + low) * steps + j, 0, 0, 0))
    in_specs = (
        [wide_spec if first else tile_spec]
        + [pl.BlockSpec((1, depth, HD), lambda k, j, s: (k + low, 0, 0))] * len(blocks)
        + [row_spec]
    )
    args = [queries if first else state[2]] + blocks + [lstart]
    scratch = [
        pltpu.SMEM((len(blocks),), jnp.int32),
    ]
    aliases = {}
    out_shape = [jax.ShapeDtypeStruct(acc_shape, F32), jax.ShapeDtypeStruct(top_shape, F32)]
    out_specs = [acc_spec, top_spec]
    if first:
        out_shape += [jax.ShapeDtypeStruct((kvl * steps, group, rows, HD), BF16)]
        out_specs += [tile_spec]
        args += [draft_kv]
        in_specs += [pl.BlockSpec((steps, 2, rows, HD), lambda k, j, s: (0, 0, 0, k + low))]
        scratch = [
            pltpu.VMEM((steps, group, rows), F32),
            pltpu.VMEM((2, rows, rows), F32),
        ] + scratch
    if state is not None:
        aliases = {len(args) + 1: 0, len(args) + 2: 1}
        if first:
            aliases[len(args) + 3] = 2
        args += state[: 3 if first else 2]
        in_specs += [pl.BlockSpec(memory_space=pl.ANY)] * 3 if first else [acc_spec, top_spec]
    if last:
        aliases = {}
        args += losses
        in_specs += [pl.BlockSpec(losses[0].shape, lambda k, j, s: (0, 0, 0))] * len(losses)
        out_shape = [
            jax.ShapeDtypeStruct(queries.shape, BF16),
            jax.ShapeDtypeStruct((steps, kvl * group, rows), F32),
            jax.ShapeDtypeStruct((1, rows), F32),
        ]
        out_specs = [
            pl.BlockSpec((1, rows, group * HD), lambda k, j, s: (j, 0, k)),
            pl.BlockSpec((1, group, rows), lambda k, j, s: (j, k, 0)),
            row_spec,
        ]
        scratch = [
            pltpu.VMEM((1, group, KEEP, rows), F32),
            pltpu.VMEM((1, 2, group, rows), F32),
        ] + scratch
    work = (high - low) * steps * group * rows * rows * len(blocks)
    return pl.pallas_call(
        functools.partial(stage_kernel, group, rows, steps, sources, first, chained, len(losses)),
        out_shape=out_shape,
        grid_spec=pltpu.PrefetchScalarGridSpec(
            num_scalar_prefetch=1,
            grid=(high - low, steps),
            in_specs=in_specs,
            out_specs=out_specs,
            scratch_shapes=scratch,
        ),
        input_output_aliases=aliases,
        name="stage_first" if first else ("stage_last" if last else "stage_mid"),
        compiler_params=pltpu.CompilerParams(vmem_limit_bytes=VMEM),
        cost_estimate=pl.CostEstimate(
            flops=4 * work * HD, transcendentals=work, bytes_accessed=4 * kvl * steps * group * HD * rows
        ),
    )(doc_ids, *args)


def loss_kernel(block, width, tgt_ref, x_ref, out_ref, all_ref):
    i = pl.program_id(0)
    first = i * block
    start_col = lax.axis_index("vocab") * width
    step = min(width, 2048)
    wide = min(width, 512)
    row_at = lax.broadcasted_iota(jnp.int32, (SUB, HD), 0)
    lane_at = lax.broadcasted_iota(jnp.int32, (SUB, HD), 1)

    @pl.loop(0, block // SUB)
    def _(b):
        here = pl.ds(pl.multiple_of(b * SUB, SUB), SUB)
        peak = x_ref[here, 0:step]
        for c in range(1, width // step):
            peak = jnp.maximum(peak, x_ref[here, c * step : (c + 1) * step])
        peak = jnp.max(peak.astype(F32), axis=1, keepdims=True)
        total = jnp.zeros((SUB, wide), F32)
        for c in range(width // wide):
            x = x_ref[here, c * wide : (c + 1) * wide].astype(F32)
            total = total + jnp.exp2((x - peak) * LOG2E)
        total = jnp.sum(total, axis=1, keepdims=True)
        hit = jnp.zeros((SUB, HD), F32)
        for r in range(SUB):
            t = tgt_ref[first + b * SUB + r] - start_col
            inside = (t >= 0) & (t < width)
            lane = jnp.where(inside, t, 0)
            start = pl.multiple_of((lane // HD) * HD, HD)
            x = x_ref[here, pl.ds(start, HD)].astype(F32)
            hit = jnp.where((row_at == r) & (lane_at == lane - start) & inside, x, hit)
        hit = jnp.sum(hit, axis=1, keepdims=True)
        there = pl.ds(pl.multiple_of(first + b * SUB, SUB), SUB)
        all_ref[there, :] = jnp.where(lane_at == 0, peak, jnp.where(lane_at == 1, total, hit))

    @pl.when(i == pl.num_programs(0) - 1)
    def _():
        out_ref[0] = all_ref[...].T[0:8]


def loss_parts(logits, targets):
    rows, width = logits.shape
    block = 64
    return pl.pallas_call(
        functools.partial(loss_kernel, block, width),
        grid_spec=pltpu.PrefetchScalarGridSpec(
            num_scalar_prefetch=1,
            grid=(rows // block,),
            in_specs=[pl.BlockSpec((block, width), lambda i, t: (i, 0))],
            out_specs=pl.BlockSpec((1, 8, rows), lambda i, t: (0, 0, 0)),
            scratch_shapes=[pltpu.VMEM((rows, HD), F32)],
        ),
        out_shape=jax.ShapeDtypeStruct((1, 8, rows), F32),
        name="loss",
        compiler_params=pltpu.CompilerParams(vmem_limit_bytes=VMEM),
        cost_estimate=pl.CostEstimate(
            flops=4 * logits.size, transcendentals=logits.size, bytes_accessed=2 * logits.size
        ),
    )(targets, logits)


def program(queries, draft_kv, doc_ids, logits, targets):
    shards = lax.axis_size("seq")
    halves = lax.axis_size("vocab")
    levels = shards // 4

    def up(x):
        return lax.ppermute(x, "seq", [(i, i + 4) for i in range(shards - 4)])

    def swap(x, bit):
        return lax.ppermute(x, "seq", [(i, i ^ bit) for i in range(shards)])

    mine, lstart = pack(draft_kv, doc_ids)
    z, x, c, d = [mine], [], [], []

    def spread(level):
        if level + 1 < levels:
            z.append(up(z[level]))
        c.append(swap(z[level], 1))
        x.append(swap(z[level], 2))
        if level > 0:
            d.append(swap(x[level - 1], 1))
        if level + 1 == levels:
            d.append(swap(z[level], 3))

    spread(0)
    parts = loss_parts(logits, targets)
    z[1], x[0], parts = lax.optimization_barrier((z[1], x[0], parts))
    spread(1)
    losses = [parts] + [
        lax.ppermute(parts, "vocab", [(i, (i + t) % halves) for i in range(halves)])
        for t in range(1, halves)
    ]

    def run(picked, state, **more):
        names = {"z": (z, 0), "c": (c, 1), "x": (x, 2), "d": (d, 3)}
        blocks = [names[name][0][level] for name, level in picked]
        sources = [(names[name][1], level) for name, level in picked]
        return stage(queries, draft_kv, doc_ids, blocks, lstart, sources, state, **more)

    kvl = draft_kv.shape[3] // HD
    cuts = [0, kvl // 2, kvl] if kvl > 1 else [0, kvl]
    state = None
    for low, high in zip(cuts, cuts[1:]):
        state = run([("z", 0), ("c", 0)], state, heads=(low, high))
        level = len(c)
        if level < levels:
            z[level], x[level - 1], top = lax.optimization_barrier((z[level], x[level - 1], state[1]))
            state = [state[0], top, state[2]]
            spread(level)
    while len(c) < levels:
        spread(len(c))
    rest = [("x", 0), ("d", 0)]
    for level in range(1, levels):
        rest += [(name, level) for name in "zcxd"]
    split = [0, 6] + list(range(14, len(rest) + 1, 8))
    for begin, end in zip(split, split[1:]):
        final = end == len(rest)
        moved = run(rest[begin:end], state, losses=losses if final else [])
        state = moved if final else [*moved, state[2]]
    out, peaks, token_loss = state
    return (out, peaks.transpose(0, 2, 1), token_loss.reshape(-1))


def solution(mesh):
    in_specs = (
        P(None, "seq", "vocab"),
        P(None, None, "seq", "vocab"),
        P("seq"),
        P("seq", "vocab"),
        P("seq"),
    )
    out_specs = (P(None, "seq", "vocab"), P(None, "seq", "vocab"), P("seq"))
    return jax.shard_map(program, mesh=mesh, in_specs=in_specs, out_specs=out_specs, check_vma=False)
```

```python
import functools

import jax
import jax.numpy as jnp
from jax import lax
from jax.experimental import pallas as pl
from jax.experimental.pallas import tpu as pltpu
from jax.sharding import PartitionSpec as P


HD = 128
SUB = 16
LOG2E = 1.4426950408889634
FILL = -1e30
NT = (((1,), (1,)), ((), ()))
LIMIT = 60.0
KEEP = HD + 8
VMEM = 67043328
F32 = jnp.float32
BF16 = jnp.bfloat16


def pack_kernel(kvl, rows, kv_ref, doc_ref, out_ref, lst_ref):
    chunks = rows // HD
    along = jnp.broadcast_to(doc_ref[...].astype(F32), (rows, rows))
    lst_ref[...] = jnp.sum(jnp.where(along.T < along, 1.0, 0.0), axis=0, keepdims=True)
    for k in range(kvl):
        cols = slice(k * HD, (k + 1) * HD)
        out_ref[k, 0:rows, :] = kv_ref[0, 0, :, cols]
        vt = kv_ref[0, 1, :, cols].astype(F32).T.astype(BF16)
        docs = doc_ref[...].astype(F32).astype(BF16)
        for h in range(chunks):
            out_ref[k, rows + h * HD : rows + (h + 1) * HD, :] = vt[:, h * HD : (h + 1) * HD]
            out_ref[k, 2 * rows + h * SUB : 2 * rows + (h + 1) * SUB, :] = jnp.broadcast_to(
                docs[:, h * HD : (h + 1) * HD], (SUB, HD)
            )


def pack(draft_kv, doc_ids):
    rows = doc_ids.shape[0]
    kvl = draft_kv.shape[3] // HD
    depth = 2 * rows + SUB * (rows // HD)
    return pl.pallas_call(
        functools.partial(pack_kernel, kvl, rows),
        grid=(1,),
        out_shape=[
            jax.ShapeDtypeStruct((kvl, depth, HD), BF16),
            jax.ShapeDtypeStruct((1, rows), F32),
        ],
        in_specs=[
            pl.BlockSpec((1, 2, rows, kvl * HD), lambda i: (0, 0, 0, 0)),
            pl.BlockSpec((1, rows), lambda i: (0, 0)),
        ],
        out_specs=[
            pl.BlockSpec((kvl, depth, HD), lambda i: (0, 0, 0)),
            pl.BlockSpec((1, rows), lambda i: (0, 0)),
        ],
        name="pack",
    )(draft_kv, doc_ids.reshape(1, rows))


def stage_kernel(group, rows, steps, sources, first, chained, losses, doc_ref, *refs):
    refs = list(refs)
    last = losses > 0
    pairs = len(sources) // 2
    q_ref = refs.pop(0)
    q_all = q_ref
    blocks = [refs.pop(0) for _ in range(2 * pairs)]
    lst_ref = refs.pop(0)
    if first:
        own_ref = refs.pop(0)
    else:
        acc_in = refs.pop(0)
        top_in = refs.pop(0)
    if chained:
        refs = refs[3:]
    loss_refs = [refs.pop(0) for _ in range(losses)]
    if last:
        out_ref, peak_ref, loss_out, acc_out, top_out, bias_ref, count_ref = refs
    elif first:
        acc_out, top_out, q_all, own_s, bias_ref, count_ref = refs
    else:
        acc_out, top_out, bias_ref, count_ref = refs
    step = pl.program_id(1)
    opening = (pl.program_id(0) == 0) & (step == 0)
    scale = HD ** (-0.5)
    c2 = scale * LOG2E
    chunks = rows // HD
    lead = lst_ref[...] == 0.0
    if first:
        for g in range(group):
            q_all[0, g] = q_ref[0, :, g * HD : (g + 1) * HD]

    @pl.when(opening)
    def _():
        me = lax.axis_index("seq")
        first_doc = doc_ref[0].astype(F32)
        for b, (flip, level) in enumerate(sources):
            source = (me ^ flip) - 4 * level
            below = jnp.zeros((SUB, HD), F32)
            for h in range(chunks):
                docs = blocks[b][0, 2 * rows + h * SUB : 2 * rows + (h + 1) * SUB, :].astype(F32)
                below = below + jnp.where(docs < first_doc, 1.0, 0.0)
            below = (jnp.sum(below) * (1.0 / SUB)).astype(jnp.int32)
            count_ref[b] = jnp.where((source >= 0) & (source < me), below, rows)

    if last:

        @pl.when(opening)
        def _():
            peak = functools.reduce(jnp.maximum, [r[0, 0:1, :] for r in loss_refs])
            total = sum(r[0, 1:2, :] * jnp.exp(r[0, 0:1, :] - peak) for r in loss_refs)
            loss_out[...] = peak + jnp.log(total) - sum(r[0, 2:3, :] for r in loss_refs)

    def values(b):
        parts = [blocks[b][0, rows + h * HD : rows + (h + 1) * HD, :] for h in range(chunks)]
        return jnp.concatenate([jnp.concatenate(parts, axis=1), jnp.ones((SUB, rows), BF16)], axis=0)

    def folded(v, op):
        return op(v.reshape(rows // 8, 8, rows), axis=0)

    def usable(pair):
        key_at = lax.broadcasted_iota(jnp.int32, (rows, rows), 0)
        ok = [key_at >= count_ref[2 * pair + i] for i in range(2)]
        if first:
            tok_at = lax.broadcasted_iota(jnp.int32, (rows, rows), 1)
            ok[0] = (key_at <= tok_at) & (key_at.astype(F32) >= lst_ref[...])
            ok[1] = ok[1] & lead
        return ok

    def scores(pair, i, q):
        return lax.dot_general(
            blocks[2 * pair + i][0, 0:rows, :], q, NT, preferred_element_type=F32
        )

    def pair_values(pair, count=2):
        return jnp.concatenate([values(2 * pair + i) for i in range(count)], axis=1)

    def visit(chosen, masked, fresh, count=2):
        units = [(g, pair) for g in range(group) for pair in chosen]
        vts = {pair: pair_values(pair, count) for pair in chosen}
        best = {}
        waiting = []
        late = 4 // count
        for n in range(len(units) + late):
            if n < len(units):
                g, pair = units[n]
                probs = []
                for i in range(count):
                    s = scores(pair, i, q_all[0, g])
                    if masked:
                        s = s + bias_ref[2 * pair + i]
                    m = folded(s, jnp.max)
                    best[g] = jnp.maximum(best[g], m) if g in best else m
                    probs.append(jnp.exp2(s * c2).astype(BF16))
                if pair == chosen[-1]:
                    peak = jnp.max(best.pop(g), axis=0, keepdims=True)
                    if not first:
                        peak = jnp.where(lead, peak, FILL)
                    top_out[0, 1, g : g + 1, :] = jnp.maximum(top_out[0, 1, g : g + 1, :], peak)
                waiting.append((g, pair, jnp.concatenate(probs, axis=0)))
            if n >= late:
                g, pair, p = waiting.pop(0)
                more = jnp.dot(vts[pair], p, preferred_element_type=F32)[0:KEEP]
                old = acc_in if fresh and pair == chosen[0] else acc_out
                acc_out[0, g] = old[0, g] + (more if first else jnp.where(lead, more, 0.0))

    def revisit(pair):
        ok = usable(pair)
        if not first:
            ok = [one & lead for one in ok]
        vt = pair_values(pair)

        @pl.loop(0, group)
        def _(g):
            shift = top_out[0, 0, pl.ds(g, 1), :] * c2
            probs = [
                jnp.exp2(jnp.where(ok[i], scores(pair, i, q_all[0, g]), FILL) * c2 - shift) for i in range(2)
            ]
            p = jnp.concatenate(probs, axis=0).astype(BF16)
            acc_out[0, g] = acc_out[0, g] + jnp.dot(vt, p, preferred_element_type=F32)[0:KEEP]

    @pl.when(opening)
    def _():
        for pair in range(pairs):
            for i, ok in enumerate(usable(pair)):
                bias_ref[2 * pair + i] = jnp.where(ok, 0.0, FILL)

    if first:

        ones = jnp.ones((SUB, HD), BF16)

        def diagonal(g, i):
            prod = q_all[0, g].astype(F32) * own_ref[i, 0].astype(F32)
            high = prod.astype(BF16)
            low = (prod - high.astype(F32)).astype(BF16)
            both = jnp.concatenate([high, low], axis=1)
            wide = jnp.concatenate([ones, ones], axis=1)
            return lax.dot_general(wide, both, NT, preferred_element_type=F32)[0:1]

        for i in range(1, steps):

            @pl.when(step >= i)
            def _():
                for g in range(group):
                    own_s[i, g : g + 1, :] = diagonal(g, i)

            @pl.when(step < i)
            def _():
                own_s[i] = jnp.full((group, rows), FILL, F32)

        top_out[0, 0] = jnp.zeros((group, rows), F32)
        top_out[0, 1] = functools.reduce(jnp.maximum, [own_s[i] for i in range(1, steps)])

        def start():
            weights = [jnp.exp2((own_s[i] - top_out[0, 0]) * c2) for i in range(1, steps)]
            for g in range(group):
                acc_out[0, g, 0:HD] = jnp.zeros((HD, rows), F32)
                acc_out[0, g, HD:KEEP] = jnp.broadcast_to(
                    functools.reduce(jnp.add, weights)[g : g + 1, :], (KEEP - HD, rows)
                )
            for i in range(1, steps):

                @pl.when(step >= i)
                def _():
                    own_val = own_ref[i, 1].astype(F32).T
                    for g in range(group):
                        w = weights[i - 1][g : g + 1, :].astype(BF16).astype(F32)
                        acc_out[0, g, 0:HD] = acc_out[0, g, 0:HD] + own_val * w

        start()

        @pl.when(count_ref[1] < rows)
        def _():
            visit([0], True, False)

        @pl.when(count_ref[1] >= rows)
        def _():
            visit([0], True, False, 1)

        spread = jnp.max(jnp.abs(top_out[0, 1])) * c2

        @pl.when(spread > LIMIT)
        def _():
            top_out[0, 0] = top_out[0, 1]
            start()
            revisit(0)

    else:
        top_out[...] = top_in[...]
        some, full = [], []
        for pair in range(pairs):
            a, b = count_ref[2 * pair], count_ref[2 * pair + 1]
            some.append(jnp.minimum(a, b) < rows)
            full.append(jnp.maximum(a, b) == 0)
        half = [count_ref[2 * pair + 1] >= rows for pair in range(pairs)]

        together = {}
        for begin in range(pairs % 2, pairs, 2):
            a, b = begin, begin + 1
            plain = begin < 2
            if plain:
                both = full[a] & full[b]
            else:
                both = some[a] & some[b] & jnp.logical_not(half[a] | half[b])
            together[a] = together[b] = both
            opens = begin < 2

            @pl.when(both)
            def _():
                visit([a, b], not plain, opens)

            if opens:

                @pl.when(jnp.logical_not(both))
                def _():
                    for g in range(group):
                        acc_out[0, g] = acc_in[0, g]

        for pair in range(pairs):
            alone = some[pair] & jnp.logical_not(together.get(pair, False))

            @pl.when(alone & jnp.logical_not(half[pair]))
            def _():
                visit([pair], True, False)

            @pl.when(alone & half[pair])
            def _():
                visit([pair], True, False, 1)

        past = top_in[0, 0]
        spread = jnp.maximum(jnp.max(top_out[0, 1]) * c2 - LIMIT, jnp.max(jnp.abs(past)))

        @pl.when(spread > 0.0)
        def _():
            top_out[0, 0] = top_out[0, 1]
            fade = jnp.exp2((past - top_out[0, 1]) * c2)
            for g in range(group):
                acc_out[0, g] = acc_in[0, g] * fade[g : g + 1, :]
            for pair in range(pairs):

                @pl.when(some[pair])
                def _():
                    revisit(pair)

    if last:
        for g in range(group):
            o = acc_out[0, g, 0:HD] * (1.0 / acc_out[0, g, HD : HD + 1])
            out_ref[0, :, g * HD : (g + 1) * HD] = o.astype(BF16).T
        peak_ref[0] = top_out[0, 1] * scale


def stage(queries, draft_kv, doc_ids, blocks, lstart, sources, state, losses=(), heads=None):
    steps, rows, width = queries.shape
    kvl = draft_kv.shape[3] // HD
    group = width // HD // kvl
    depth = blocks[0].shape[1]
    first = heads is not None
    low, high = heads if first else (0, kvl)
    chained = first and state is not None
    last = len(losses) > 0
    acc_shape = (kvl * steps, group, KEEP, rows)
    top_shape = (kvl * steps, 2, group, rows)
    acc_spec = pl.BlockSpec((1, group, KEEP, rows), lambda k, j, s: ((k + low) * steps + j, 0, 0, 0))
    top_spec = pl.BlockSpec((1, 2, group, rows), lambda k, j, s: ((k + low) * steps + j, 0, 0, 0))
    row_spec = pl.BlockSpec((1, rows), lambda k, j, s: (0, 0))
    wide_spec = pl.BlockSpec((1, rows, group * HD), lambda k, j, s: (j, 0, k + low))
    tile_spec = pl.BlockSpec((1, group, rows, HD), lambda k, j, s: ((k + low) * steps + j, 0, 0, 0))
    in_specs = (
        [wide_spec if first else tile_spec]
        + [pl.BlockSpec((1, depth, HD), lambda k, j, s: (k + low, 0, 0))] * len(blocks)
        + [row_spec]
    )
    args = [queries if first else state[2]] + blocks + [lstart]
    scratch = [
        pltpu.VMEM((len(blocks), rows, rows), F32),
        pltpu.SMEM((len(blocks),), jnp.int32),
    ]
    aliases = {}
    out_shape = [jax.ShapeDtypeStruct(acc_shape, F32), jax.ShapeDtypeStruct(top_shape, F32)]
    out_specs = [acc_spec, top_spec]
    if first:
        out_shape += [jax.ShapeDtypeStruct((kvl * steps, group, rows, HD), BF16)]
        out_specs += [tile_spec]
        args += [draft_kv]
        in_specs += [pl.BlockSpec((steps, 2, rows, HD), lambda k, j, s: (0, 0, 0, k + low))]
        scratch = [
            pltpu.VMEM((steps, group, rows), F32),
        ] + scratch
    if state is not None:
        aliases = {len(args) + 1: 0, len(args) + 2: 1}
        if first:
            aliases[len(args) + 3] = 2
        args += state[: 3 if first else 2]
        in_specs += [pl.BlockSpec(memory_space=pl.ANY)] * 3 if first else [acc_spec, top_spec]
    if last:
        aliases = {}
        args += losses
        in_specs += [pl.BlockSpec(losses[0].shape, lambda k, j, s: (0, 0, 0))] * len(losses)
        out_shape = [
            jax.ShapeDtypeStruct(queries.shape, BF16),
            jax.ShapeDtypeStruct((steps, kvl * group, rows), F32),
            jax.ShapeDtypeStruct((1, rows), F32),
        ]
        out_specs = [
            pl.BlockSpec((1, rows, group * HD), lambda k, j, s: (j, 0, k)),
            pl.BlockSpec((1, group, rows), lambda k, j, s: (j, k, 0)),
            row_spec,
        ]
        scratch = [
            pltpu.VMEM((1, group, KEEP, rows), F32),
            pltpu.VMEM((1, 2, group, rows), F32),
        ] + scratch
    work = (high - low) * steps * group * rows * rows * len(blocks)
    return pl.pallas_call(
        functools.partial(
            stage_kernel, group, rows, steps, sources, first, chained, len(losses)
        ),
        out_shape=out_shape,
        grid_spec=pltpu.PrefetchScalarGridSpec(
            num_scalar_prefetch=1,
            grid=(high - low, steps),
            in_specs=in_specs,
            out_specs=out_specs,
            scratch_shapes=scratch,
        ),
        input_output_aliases=aliases,
        name="stage_first" if first else ("stage_last" if last else "stage_mid"),
        compiler_params=pltpu.CompilerParams(vmem_limit_bytes=VMEM),
        cost_estimate=pl.CostEstimate(
            flops=4 * work * HD, transcendentals=work, bytes_accessed=4 * kvl * steps * group * HD * rows
        ),
    )(doc_ids, *args)


def loss_kernel(block, width, tgt_ref, x_ref, out_ref, all_ref):
    i = pl.program_id(0)
    first = i * block
    start_col = lax.axis_index("vocab") * width
    step = min(width, 2048)
    wide = min(width, 512)
    row_at = lax.broadcasted_iota(jnp.int32, (SUB, HD), 0)
    lane_at = lax.broadcasted_iota(jnp.int32, (SUB, HD), 1)

    @pl.loop(0, block // SUB)
    def _(b):
        here = pl.ds(pl.multiple_of(b * SUB, SUB), SUB)
        peak = x_ref[here, 0:step]
        for c in range(1, width // step):
            peak = jnp.maximum(peak, x_ref[here, c * step : (c + 1) * step])
        peak = jnp.max(peak.astype(F32), axis=1, keepdims=True)
        total = jnp.zeros((SUB, wide), F32)
        for c in range(width // wide):
            x = x_ref[here, c * wide : (c + 1) * wide].astype(F32)
            total = total + jnp.exp2((x - peak) * LOG2E)
        total = jnp.sum(total, axis=1, keepdims=True)
        hit = jnp.zeros((SUB, HD), F32)
        for r in range(SUB):
            t = tgt_ref[first + b * SUB + r] - start_col
            inside = (t >= 0) & (t < width)
            lane = jnp.where(inside, t, 0)
            start = pl.multiple_of((lane // HD) * HD, HD)
            x = x_ref[here, pl.ds(start, HD)].astype(F32)
            hit = jnp.where((row_at == r) & (lane_at == lane - start) & inside, x, hit)
        hit = jnp.sum(hit, axis=1, keepdims=True)
        there = pl.ds(pl.multiple_of(first + b * SUB, SUB), SUB)
        all_ref[there, :] = jnp.where(lane_at == 0, peak, jnp.where(lane_at == 1, total, hit))

    @pl.when(i == pl.num_programs(0) - 1)
    def _():
        out_ref[0] = all_ref[...].T[0:8]


def loss_parts(logits, targets):
    rows, width = logits.shape
    block = 64
    return pl.pallas_call(
        functools.partial(loss_kernel, block, width),
        grid_spec=pltpu.PrefetchScalarGridSpec(
            num_scalar_prefetch=1,
            grid=(rows // block,),
            in_specs=[pl.BlockSpec((block, width), lambda i, t: (i, 0))],
            out_specs=pl.BlockSpec((1, 8, rows), lambda i, t: (0, 0, 0)),
            scratch_shapes=[pltpu.VMEM((rows, HD), F32)],
        ),
        out_shape=jax.ShapeDtypeStruct((1, 8, rows), F32),
        name="loss",
        compiler_params=pltpu.CompilerParams(vmem_limit_bytes=VMEM),
        cost_estimate=pl.CostEstimate(
            flops=4 * logits.size, transcendentals=logits.size, bytes_accessed=2 * logits.size
        ),
    )(targets, logits)


def program(queries, draft_kv, doc_ids, logits, targets):
    shards = lax.axis_size("seq")
    halves = lax.axis_size("vocab")
    levels = shards // 4

    def up(x):
        return lax.ppermute(x, "seq", [(i, i + 4) for i in range(shards - 4)])

    def swap(x, bit):
        return lax.ppermute(x, "seq", [(i, i ^ bit) for i in range(shards)])

    mine, lstart = pack(draft_kv, doc_ids)
    z, x, c, d = [mine], [], [], []

    def spread(level):
        if level + 1 < levels:
            z.append(up(z[level]))
        c.append(swap(z[level], 1))
        x.append(swap(z[level], 2))
        if level > 0:
            d.append(swap(x[level - 1], 1))
        if level + 1 == levels:
            d.append(swap(z[level], 3))

    spread(0)
    parts = loss_parts(logits, targets)
    z[1], x[0], parts = lax.optimization_barrier((z[1], x[0], parts))
    spread(1)
    losses = [parts] + [
        lax.ppermute(parts, "vocab", [(i, (i + t) % halves) for i in range(halves)])
        for t in range(1, halves)
    ]

    def run(picked, state, **more):
        names = {"z": (z, 0), "c": (c, 1), "x": (x, 2), "d": (d, 3)}
        blocks = [names[name][0][level] for name, level in picked]
        sources = [(names[name][1], level) for name, level in picked]
        return stage(queries, draft_kv, doc_ids, blocks, lstart, sources, state, **more)

    kvl = draft_kv.shape[3] // HD
    cuts = [0, kvl // 2, kvl] if kvl > 1 else [0, kvl]
    state = None
    for low, high in zip(cuts, cuts[1:]):
        state = run([("z", 0), ("c", 0)], state, heads=(low, high))
        level = len(c)
        if level < levels:
            z[level], x[level - 1], top = lax.optimization_barrier((z[level], x[level - 1], state[1]))
            state = [state[0], top, state[2]]
            spread(level)
    while len(c) < levels:
        spread(len(c))
    rest = [("x", 0), ("d", 0)]
    for level in range(1, levels):
        rest += [(name, level) for name in "zcxd"]
    split = [0, 6] + list(range(14, len(rest) + 1, 8))
    for begin, end in zip(split, split[1:]):
        final = end == len(rest)
        moved = run(rest[begin:end], state, losses=losses if final else [])
        state = moved if final else [*moved, state[2]]
    out, peaks, token_loss = state
    return (out, peaks.transpose(0, 2, 1), token_loss.reshape(-1))


def solution(mesh):
    in_specs = (
        P(None, "seq", "vocab"),
        P(None, None, "seq", "vocab"),
        P("seq"),
        P("seq", "vocab"),
        P("seq"),
    )
    out_specs = (P(None, "seq", "vocab"), P(None, "seq", "vocab"), P("seq"))
    return jax.shard_map(program, mesh=mesh, in_specs=in_specs, out_specs=out_specs, check_vma=False)
```

```python
import functools

import jax
import jax.numpy as jnp
from jax import lax
from jax.experimental import pallas as pl
from jax.experimental.pallas import tpu as pltpu
from jax.sharding import PartitionSpec as P


HD = 128
SUB = 16
LOG2E = 1.4426950408889634
FILL = -1e30
NT = (((1,), (1,)), ((), ()))
LIMIT = 60.0
KEEP = HD + 8
VMEM = 67043328
F32 = jnp.float32
BF16 = jnp.bfloat16


def pack_kernel(kvl, rows, kv_ref, doc_ref, out_ref, lst_ref):
    chunks = rows // HD
    along = jnp.broadcast_to(doc_ref[...].astype(F32), (rows, rows))
    lst_ref[...] = jnp.sum(jnp.where(along.T < along, 1.0, 0.0), axis=0, keepdims=True)
    for k in range(kvl):
        cols = slice(k * HD, (k + 1) * HD)
        out_ref[k, 0:rows, :] = kv_ref[0, 0, :, cols]
        vt = kv_ref[0, 1, :, cols].astype(F32).T.astype(BF16)
        docs = doc_ref[...].astype(F32).astype(BF16)
        for h in range(chunks):
            out_ref[k, rows + h * HD : rows + (h + 1) * HD, :] = vt[:, h * HD : (h + 1) * HD]
            out_ref[k, 2 * rows + h * SUB : 2 * rows + (h + 1) * SUB, :] = jnp.broadcast_to(
                docs[:, h * HD : (h + 1) * HD], (SUB, HD)
            )


def pack(draft_kv, doc_ids):
    rows = doc_ids.shape[0]
    kvl = draft_kv.shape[3] // HD
    depth = 2 * rows + SUB * (rows // HD)
    return pl.pallas_call(
        functools.partial(pack_kernel, kvl, rows),
        grid=(1,),
        out_shape=[
            jax.ShapeDtypeStruct((kvl, depth, HD), BF16),
            jax.ShapeDtypeStruct((1, rows), F32),
        ],
        in_specs=[
            pl.BlockSpec((1, 2, rows, kvl * HD), lambda i: (0, 0, 0, 0)),
            pl.BlockSpec((1, rows), lambda i: (0, 0)),
        ],
        out_specs=[
            pl.BlockSpec((kvl, depth, HD), lambda i: (0, 0, 0)),
            pl.BlockSpec((1, rows), lambda i: (0, 0)),
        ],
        name="pack",
    )(draft_kv, doc_ids.reshape(1, rows))


def stage_kernel(group, rows, steps, sources, first, chained, losses, doc_ref, *refs):
    refs = list(refs)
    last = losses > 0
    pairs = len(sources) // 2
    q_ref = refs.pop(0)
    q_all = q_ref
    blocks = [refs.pop(0) for _ in range(2 * pairs)]
    lst_ref = refs.pop(0)
    if first:
        own_ref = refs.pop(0)
    else:
        acc_in = refs.pop(0)
        top_in = refs.pop(0)
    if chained:
        refs = refs[3:]
    loss_refs = [refs.pop(0) for _ in range(losses)]
    if last:
        out_ref, peak_ref, loss_out, acc_out, top_out, bias_ref, count_ref = refs
    elif first:
        acc_out, top_out, q_all, own_s, bias_ref, count_ref = refs
    else:
        acc_out, top_out, bias_ref, count_ref = refs
    step = pl.program_id(1)
    opening = (pl.program_id(0) == 0) & (step == 0)
    scale = HD ** (-0.5)
    c2 = scale * LOG2E
    chunks = rows // HD
    lead = lst_ref[...] == 0.0
    if first:
        for g in range(group):
            q_all[0, g] = q_ref[0, :, g * HD : (g + 1) * HD]

    @pl.when(opening)
    def _():
        me = lax.axis_index("seq")
        first_doc = doc_ref[0].astype(F32)
        for b, (flip, level) in enumerate(sources):
            source = (me ^ flip) - 4 * level
            below = jnp.zeros((SUB, HD), F32)
            for h in range(chunks):
                docs = blocks[b][0, 2 * rows + h * SUB : 2 * rows + (h + 1) * SUB, :].astype(F32)
                below = below + jnp.where(docs < first_doc, 1.0, 0.0)
            below = (jnp.sum(below) * (1.0 / SUB)).astype(jnp.int32)
            count_ref[b] = jnp.where((source >= 0) & (source < me), below, rows)

    if last:

        @pl.when(opening)
        def _():
            peak = functools.reduce(jnp.maximum, [r[0, 0:1, :] for r in loss_refs])
            total = sum(r[0, 1:2, :] * jnp.exp(r[0, 0:1, :] - peak) for r in loss_refs)
            loss_out[...] = peak + jnp.log(total) - sum(r[0, 2:3, :] for r in loss_refs)

    def values(b):
        parts = [blocks[b][0, rows + h * HD : rows + (h + 1) * HD, :] for h in range(chunks)]
        return jnp.concatenate([jnp.concatenate(parts, axis=1), jnp.ones((SUB, rows), BF16)], axis=0)

    def folded(v, op):
        return op(v.reshape(rows // 8, 8, rows), axis=0)

    def usable(pair):
        key_at = lax.broadcasted_iota(jnp.int32, (rows, rows), 0)
        ok = [key_at >= count_ref[2 * pair + i] for i in range(2)]
        if first:
            tok_at = lax.broadcasted_iota(jnp.int32, (rows, rows), 1)
            ok[0] = (key_at <= tok_at) & (key_at.astype(F32) >= lst_ref[...])
            ok[1] = ok[1] & lead
        return ok

    def scores(pair, i, q):
        return lax.dot_general(
            blocks[2 * pair + i][0, 0:rows, :], q, NT, preferred_element_type=F32
        )

    def pair_values(pair, count=2):
        return jnp.concatenate([values(2 * pair + i) for i in range(count)], axis=1)

    def visit(chosen, masked, fresh, count=2):
        units = [(g, pair) for g in range(group) for pair in chosen]
        vts = {pair: pair_values(pair, count) for pair in chosen}
        best = {}
        waiting = []
        late = 4 // count
        for n in range(len(units) + late):
            if n < len(units):
                g, pair = units[n]
                probs = []
                for i in range(count):
                    s = scores(pair, i, q_all[0, g])
                    if masked:
                        s = s + bias_ref[2 * pair + i]
                    m = folded(s, jnp.max)
                    best[g] = jnp.maximum(best[g], m) if g in best else m
                    probs.append(jnp.exp2(s * c2).astype(BF16))
                if pair == chosen[-1]:
                    peak = jnp.max(best.pop(g), axis=0, keepdims=True)
                    if not first:
                        peak = jnp.where(lead, peak, FILL)
                    top_out[0, 1, g : g + 1, :] = jnp.maximum(top_out[0, 1, g : g + 1, :], peak)
                waiting.append((g, pair, jnp.concatenate(probs, axis=0)))
            if n >= late:
                g, pair, p = waiting.pop(0)
                more = jnp.dot(vts[pair], p, preferred_element_type=F32)[0:KEEP]
                old = acc_in if fresh and pair == chosen[0] else acc_out
                acc_out[0, g] = old[0, g] + (more if first else jnp.where(lead, more, 0.0))

    def revisit(pair):
        ok = usable(pair)
        if not first:
            ok = [one & lead for one in ok]
        vt = pair_values(pair)

        @pl.loop(0, group)
        def _(g):
            shift = top_out[0, 0, pl.ds(g, 1), :] * c2
            probs = [
                jnp.exp2(jnp.where(ok[i], scores(pair, i, q_all[0, g]), FILL) * c2 - shift) for i in range(2)
            ]
            p = jnp.concatenate(probs, axis=0).astype(BF16)
            acc_out[0, g] = acc_out[0, g] + jnp.dot(vt, p, preferred_element_type=F32)[0:KEEP]

    @pl.when(opening)
    def _():
        for pair in range(pairs):
            for i, ok in enumerate(usable(pair)):
                bias_ref[2 * pair + i] = jnp.where(ok, 0.0, FILL)

    if first:

        ones = jnp.ones((SUB, HD), BF16)

        def diagonal(g, i):
            prod = q_all[0, g].astype(F32) * own_ref[i, 0].astype(F32)
            high = prod.astype(BF16)
            low = (prod - high.astype(F32)).astype(BF16)
            both = jnp.concatenate([high, low], axis=1)
            wide = jnp.concatenate([ones, ones], axis=1)
            return lax.dot_general(wide, both, NT, preferred_element_type=F32)[0:1]

        for i in range(1, steps):

            @pl.when(step >= i)
            def _():
                for g in range(group):
                    own_s[i, g : g + 1, :] = diagonal(g, i)

            @pl.when(step < i)
            def _():
                own_s[i] = jnp.full((group, rows), FILL, F32)

        top_out[0, 0] = jnp.zeros((group, rows), F32)
        top_out[0, 1] = functools.reduce(jnp.maximum, [own_s[i] for i in range(1, steps)])

        def start():
            weights = [jnp.exp2((own_s[i] - top_out[0, 0]) * c2) for i in range(1, steps)]
            for g in range(group):
                acc_out[0, g, 0:HD] = jnp.zeros((HD, rows), F32)
                acc_out[0, g, HD:KEEP] = jnp.broadcast_to(
                    functools.reduce(jnp.add, weights)[g : g + 1, :], (KEEP - HD, rows)
                )
            for i in range(1, steps):

                @pl.when(step >= i)
                def _():
                    own_val = own_ref[i, 1].astype(F32).T
                    for g in range(group):
                        w = weights[i - 1][g : g + 1, :].astype(BF16).astype(F32)
                        acc_out[0, g, 0:HD] = acc_out[0, g, 0:HD] + own_val * w

        start()

        @pl.when(count_ref[1] < rows)
        def _():
            visit([0], True, False)

        @pl.when(count_ref[1] >= rows)
        def _():
            visit([0], True, False, 1)

        spread = jnp.max(jnp.abs(top_out[0, 1])) * c2

        @pl.when(spread > LIMIT)
        def _():
            top_out[0, 0] = top_out[0, 1]
            start()
            revisit(0)

    else:
        top_out[...] = top_in[...]
        some, full = [], []
        for pair in range(pairs):
            a, b = count_ref[2 * pair], count_ref[2 * pair + 1]
            some.append(jnp.minimum(a, b) < rows)
            full.append(jnp.maximum(a, b) == 0)
        half = [count_ref[2 * pair + 1] >= rows for pair in range(pairs)]

        together = {}
        for begin in range(pairs % 2, pairs, 2):
            a, b = begin, begin + 1
            plain = begin < 2
            trio = jnp.logical_and(pairs == 3, full[0] & full[1] & full[pairs - 1])
            if plain:
                both = full[a] & full[b] & jnp.logical_not(trio)
            else:
                both = some[a] & some[b] & jnp.logical_not(half[a] | half[b])
            together[a] = together[b] = both
            opens = begin < 2

            @pl.when(both)
            def _():
                visit([a, b], not plain, opens)

            if pairs == 3:

                @pl.when(trio)
                def _():
                    visit([0, 1, 2], False, True)

                together = {pair: both | trio if pair else trio for pair in range(3)}

            if opens:

                @pl.when(jnp.logical_not(both | trio))
                def _():
                    for g in range(group):
                        acc_out[0, g] = acc_in[0, g]

        for pair in range(pairs):
            alone = some[pair] & jnp.logical_not(together.get(pair, False))

            @pl.when(alone & jnp.logical_not(half[pair]))
            def _():
                visit([pair], True, False)

            @pl.when(alone & half[pair])
            def _():
                visit([pair], True, False, 1)

        past = top_in[0, 0]
        spread = jnp.maximum(jnp.max(top_out[0, 1]) * c2 - LIMIT, jnp.max(jnp.abs(past)))

        @pl.when(spread > 0.0)
        def _():
            top_out[0, 0] = top_out[0, 1]
            fade = jnp.exp2((past - top_out[0, 1]) * c2)
            for g in range(group):
                acc_out[0, g] = acc_in[0, g] * fade[g : g + 1, :]
            for pair in range(pairs):

                @pl.when(some[pair])
                def _():
                    revisit(pair)

    if last:
        for g in range(group):
            o = acc_out[0, g, 0:HD] * (1.0 / acc_out[0, g, HD : HD + 1])
            out_ref[0, :, g * HD : (g + 1) * HD] = o.astype(BF16).T
        peak_ref[0] = top_out[0, 1] * scale


def stage(queries, draft_kv, doc_ids, blocks, lstart, sources, state, losses=(), heads=None):
    steps, rows, width = queries.shape
    kvl = draft_kv.shape[3] // HD
    group = width // HD // kvl
    depth = blocks[0].shape[1]
    first = heads is not None
    low, high = heads if first else (0, kvl)
    chained = first and state is not None
    last = len(losses) > 0
    acc_shape = (kvl * steps, group, KEEP, rows)
    top_shape = (kvl * steps, 2, group, rows)
    acc_spec = pl.BlockSpec((1, group, KEEP, rows), lambda k, j, s: ((k + low) * steps + j, 0, 0, 0))
    top_spec = pl.BlockSpec((1, 2, group, rows), lambda k, j, s: ((k + low) * steps + j, 0, 0, 0))
    row_spec = pl.BlockSpec((1, rows), lambda k, j, s: (0, 0))
    wide_spec = pl.BlockSpec((1, rows, group * HD), lambda k, j, s: (j, 0, k + low))
    tile_spec = pl.BlockSpec((1, group, rows, HD), lambda k, j, s: ((k + low) * steps + j, 0, 0, 0))
    in_specs = (
        [wide_spec if first else tile_spec]
        + [pl.BlockSpec((1, depth, HD), lambda k, j, s: (k + low, 0, 0))] * len(blocks)
        + [row_spec]
    )
    args = [queries if first else state[2]] + blocks + [lstart]
    scratch = [
        pltpu.VMEM((len(blocks), rows, rows), F32),
        pltpu.SMEM((len(blocks),), jnp.int32),
    ]
    aliases = {}
    out_shape = [jax.ShapeDtypeStruct(acc_shape, F32), jax.ShapeDtypeStruct(top_shape, F32)]
    out_specs = [acc_spec, top_spec]
    if first:
        out_shape += [jax.ShapeDtypeStruct((kvl * steps, group, rows, HD), BF16)]
        out_specs += [tile_spec]
        args += [draft_kv]
        in_specs += [pl.BlockSpec((steps, 2, rows, HD), lambda k, j, s: (0, 0, 0, k + low))]
        scratch = [
            pltpu.VMEM((steps, group, rows), F32),
        ] + scratch
    if state is not None:
        aliases = {len(args) + 1: 0, len(args) + 2: 1}
        if first:
            aliases[len(args) + 3] = 2
        args += state[: 3 if first else 2]
        in_specs += [pl.BlockSpec(memory_space=pl.ANY)] * 3 if first else [acc_spec, top_spec]
    if last:
        aliases = {}
        args += losses
        in_specs += [pl.BlockSpec(losses[0].shape, lambda k, j, s: (0, 0, 0))] * len(losses)
        out_shape = [
            jax.ShapeDtypeStruct(queries.shape, BF16),
            jax.ShapeDtypeStruct((steps, kvl * group, rows), F32),
            jax.ShapeDtypeStruct((1, rows), F32),
        ]
        out_specs = [
            pl.BlockSpec((1, rows, group * HD), lambda k, j, s: (j, 0, k)),
            pl.BlockSpec((1, group, rows), lambda k, j, s: (j, k, 0)),
            row_spec,
        ]
        scratch = [
            pltpu.VMEM((1, group, KEEP, rows), F32),
            pltpu.VMEM((1, 2, group, rows), F32),
        ] + scratch
    work = (high - low) * steps * group * rows * rows * len(blocks)
    return pl.pallas_call(
        functools.partial(
            stage_kernel, group, rows, steps, sources, first, chained, len(losses)
        ),
        out_shape=out_shape,
        grid_spec=pltpu.PrefetchScalarGridSpec(
            num_scalar_prefetch=1,
            grid=(high - low, steps),
            in_specs=in_specs,
            out_specs=out_specs,
            scratch_shapes=scratch,
        ),
        input_output_aliases=aliases,
        name="stage_first" if first else ("stage_last" if last else "stage_mid"),
        compiler_params=pltpu.CompilerParams(vmem_limit_bytes=VMEM),
        cost_estimate=pl.CostEstimate(
            flops=4 * work * HD, transcendentals=work, bytes_accessed=4 * kvl * steps * group * HD * rows
        ),
    )(doc_ids, *args)


def loss_kernel(block, width, tgt_ref, x_ref, out_ref, all_ref):
    i = pl.program_id(0)
    first = i * block
    start_col = lax.axis_index("vocab") * width
    step = min(width, 2048)
    wide = min(width, 512)
    row_at = lax.broadcasted_iota(jnp.int32, (SUB, HD), 0)
    lane_at = lax.broadcasted_iota(jnp.int32, (SUB, HD), 1)

    @pl.loop(0, block // SUB)
    def _(b):
        here = pl.ds(pl.multiple_of(b * SUB, SUB), SUB)
        peak = x_ref[here, 0:step]
        total = jnp.zeros((SUB, wide), F32)
        for c in range(width // step):
            x = x_ref[here, c * step : (c + 1) * step]
            peak = jnp.maximum(peak, x)
            for h in range(step // wide):
                total = total + jnp.exp2(x[:, h * wide : (h + 1) * wide].astype(F32) * LOG2E)
        peak = jnp.max(peak.astype(F32), axis=1, keepdims=True)
        total = jnp.sum(total, axis=1, keepdims=True)
        near = jnp.zeros((SUB, HD), F32)
        spot = jnp.full((SUB, HD), -1, jnp.int32)
        for r in range(SUB):
            t = tgt_ref[first + b * SUB + r] - start_col
            inside = (t >= 0) & (t < width)
            lane = jnp.where(inside, t, 0)
            start = pl.multiple_of((lane // HD) * HD, HD)
            near = jnp.where(row_at == r, x_ref[here, pl.ds(start, HD)].astype(F32), near)
            spot = jnp.where(row_at == r, jnp.where(inside, lane - start, -1), spot)
        hit = jnp.sum(jnp.where(lane_at == spot, near, 0.0), axis=1, keepdims=True)
        there = pl.ds(pl.multiple_of(first + b * SUB, SUB), SUB)
        all_ref[there, :] = jnp.where(lane_at == 1, total, jnp.where(lane_at == 2, hit, 0.0))

        @pl.when(jnp.max(jnp.abs(peak)) * LOG2E > LIMIT)
        def _():
            exact = jnp.zeros((SUB, wide), F32)
            for c in range(width // wide):
                x = x_ref[here, c * wide : (c + 1) * wide].astype(F32)
                exact = exact + jnp.exp2((x - peak) * LOG2E)
            exact = jnp.sum(exact, axis=1, keepdims=True)
            all_ref[there, :] = jnp.where(lane_at == 0, peak, jnp.where(lane_at == 1, exact, hit))

    @pl.when(i == pl.num_programs(0) - 1)
    def _():
        out_ref[0] = all_ref[...].T[0:8]


def loss_parts(logits, targets):
    rows, width = logits.shape
    block = 64
    return pl.pallas_call(
        functools.partial(loss_kernel, block, width),
        grid_spec=pltpu.PrefetchScalarGridSpec(
            num_scalar_prefetch=1,
            grid=(rows // block,),
            in_specs=[pl.BlockSpec((block, width), lambda i, t: (i, 0))],
            out_specs=pl.BlockSpec((1, 8, rows), lambda i, t: (0, 0, 0)),
            scratch_shapes=[pltpu.VMEM((rows, HD), F32)],
        ),
        out_shape=jax.ShapeDtypeStruct((1, 8, rows), F32),
        name="loss",
        compiler_params=pltpu.CompilerParams(vmem_limit_bytes=VMEM),
        cost_estimate=pl.CostEstimate(
            flops=4 * logits.size, transcendentals=logits.size, bytes_accessed=2 * logits.size
        ),
    )(targets, logits)


def program(queries, draft_kv, doc_ids, logits, targets):
    shards = lax.axis_size("seq")
    halves = lax.axis_size("vocab")
    levels = shards // 4

    def up(x):
        return lax.ppermute(x, "seq", [(i, i + 4) for i in range(shards - 4)])

    def swap(x, bit):
        return lax.ppermute(x, "seq", [(i, i ^ bit) for i in range(shards)])

    mine, lstart = pack(draft_kv, doc_ids)
    z, x, c, d = [mine], [], [], []

    def spread(level):
        if level + 1 < levels:
            z.append(up(z[level]))
        c.append(swap(z[level], 1))
        x.append(swap(z[level], 2))
        if level > 0:
            d.append(swap(x[level - 1], 1))
        if level + 1 == levels:
            d.append(swap(z[level], 3))

    spread(0)
    parts = loss_parts(logits, targets)
    z[1], x[0], parts = lax.optimization_barrier((z[1], x[0], parts))
    spread(1)
    losses = [parts] + [
        lax.ppermute(parts, "vocab", [(i, (i + t) % halves) for i in range(halves)])
        for t in range(1, halves)
    ]

    def run(picked, state, **more):
        names = {"z": (z, 0), "c": (c, 1), "x": (x, 2), "d": (d, 3)}
        blocks = [names[name][0][level] for name, level in picked]
        sources = [(names[name][1], level) for name, level in picked]
        return stage(queries, draft_kv, doc_ids, blocks, lstart, sources, state, **more)

    kvl = draft_kv.shape[3] // HD
    cuts = [0, kvl // 2, kvl] if kvl > 1 else [0, kvl]
    state = None
    for low, high in zip(cuts, cuts[1:]):
        state = run([("z", 0), ("c", 0)], state, heads=(low, high))
        level = len(c)
        if level < levels:
            z[level], x[level - 1], top = lax.optimization_barrier((z[level], x[level - 1], state[1]))
            state = [state[0], top, state[2]]
            spread(level)
    while len(c) < levels:
        spread(len(c))
    rest = [("x", 0), ("d", 0)]
    for level in range(1, levels):
        rest += [(name, level) for name in "zcxd"]
    split = [0, 6] + list(range(14, len(rest) + 1, 8))
    for begin, end in zip(split, split[1:]):
        final = end == len(rest)
        moved = run(rest[begin:end], state, losses=losses if final else [])
        state = moved if final else [*moved, state[2]]
    out, peaks, token_loss = state
    return (out, peaks.transpose(0, 2, 1), token_loss.reshape(-1))


def solution(mesh):
    in_specs = (
        P(None, "seq", "vocab"),
        P(None, None, "seq", "vocab"),
        P("seq"),
        P("seq", "vocab"),
        P("seq"),
    )
    out_specs = (P(None, "seq", "vocab"), P(None, "seq", "vocab"), P("seq"))
    return jax.shard_map(program, mesh=mesh, in_specs=in_specs, out_specs=out_specs, check_vma=False)
```

```python
import functools

import jax
import jax.numpy as jnp
from jax import lax
from jax.experimental import pallas as pl
from jax.experimental.pallas import tpu as pltpu
from jax.sharding import PartitionSpec as P


HD = 128
SUB = 16
LOG2E = 1.4426950408889634
FILL = -1e30
NT = (((1,), (1,)), ((), ()))
LIMIT = 60.0
KEEP = HD + 8
VMEM = 67043328
F32 = jnp.float32
BF16 = jnp.bfloat16


def pack_kernel(kvl, rows, kv_ref, doc_ref, out_ref, lst_ref):
    chunks = rows // HD
    along = jnp.broadcast_to(doc_ref[...].astype(F32), (rows, rows))
    lst_ref[...] = jnp.sum(jnp.where(along.T < along, 1.0, 0.0), axis=0, keepdims=True)
    for k in range(kvl):
        cols = slice(k * HD, (k + 1) * HD)
        out_ref[k, 0:rows, :] = kv_ref[0, 0, :, cols]
        vt = kv_ref[0, 1, :, cols].astype(F32).T.astype(BF16)
        docs = doc_ref[...].astype(F32).astype(BF16)
        for h in range(chunks):
            out_ref[k, rows + h * HD : rows + (h + 1) * HD, :] = vt[:, h * HD : (h + 1) * HD]
            out_ref[k, 2 * rows + h * SUB : 2 * rows + (h + 1) * SUB, :] = jnp.broadcast_to(
                docs[:, h * HD : (h + 1) * HD], (SUB, HD)
            )


def pack(draft_kv, doc_ids):
    rows = doc_ids.shape[0]
    kvl = draft_kv.shape[3] // HD
    depth = 2 * rows + SUB * (rows // HD)
    return pl.pallas_call(
        functools.partial(pack_kernel, kvl, rows),
        grid=(1,),
        out_shape=[
            jax.ShapeDtypeStruct((kvl, depth, HD), BF16),
            jax.ShapeDtypeStruct((1, rows), F32),
        ],
        in_specs=[
            pl.BlockSpec((1, 2, rows, kvl * HD), lambda i: (0, 0, 0, 0)),
            pl.BlockSpec((1, rows), lambda i: (0, 0)),
        ],
        out_specs=[
            pl.BlockSpec((kvl, depth, HD), lambda i: (0, 0, 0)),
            pl.BlockSpec((1, rows), lambda i: (0, 0)),
        ],
        name="pack",
    )(draft_kv, doc_ids.reshape(1, rows))


def stage_kernel(group, rows, steps, sources, first, chained, losses, doc_ref, *refs):
    refs = list(refs)
    last = losses > 0
    pairs = len(sources) // 2
    q_ref = refs.pop(0)
    q_all = q_ref
    blocks = [refs.pop(0) for _ in range(2 * pairs)]
    lst_ref = refs.pop(0)
    if first:
        own_ref = refs.pop(0)
    else:
        acc_in = refs.pop(0)
        top_in = refs.pop(0)
    if chained:
        refs = refs[3:]
    loss_refs = [refs.pop(0) for _ in range(losses)]
    if last:
        out_ref, peak_ref, loss_out, acc_out, top_out, bias_ref, count_ref = refs
    elif first:
        acc_out, top_out, q_all, own_s, bias_ref, count_ref = refs
    else:
        acc_out, top_out, bias_ref, count_ref = refs
    step = pl.program_id(1)
    opening = (pl.program_id(0) == 0) & (step == 0)
    scale = HD ** (-0.5)
    c2 = scale * LOG2E
    chunks = rows // HD
    lead = lst_ref[...] == 0.0
    if first:
        for g in range(group):
            q_all[0, g] = q_ref[0, :, g * HD : (g + 1) * HD]

    @pl.when(opening)
    def _():
        me = lax.axis_index("seq")
        first_doc = doc_ref[0].astype(F32)
        for b, (flip, level) in enumerate(sources):
            source = (me ^ flip) - 4 * level
            below = jnp.zeros((SUB, HD), F32)
            for h in range(chunks):
                docs = blocks[b][0, 2 * rows + h * SUB : 2 * rows + (h + 1) * SUB, :].astype(F32)
                below = below + jnp.where(docs < first_doc, 1.0, 0.0)
            below = (jnp.sum(below) * (1.0 / SUB)).astype(jnp.int32)
            count_ref[b] = jnp.where((source >= 0) & (source < me), below, rows)

    if last:

        @pl.when(opening)
        def _():
            peak = functools.reduce(jnp.maximum, [r[0, 0:1, :] for r in loss_refs])
            total = sum(r[0, 1:2, :] * jnp.exp(r[0, 0:1, :] - peak) for r in loss_refs)
            loss_out[...] = peak + jnp.log(total) - sum(r[0, 2:3, :] for r in loss_refs)

    def values(b):
        parts = [blocks[b][0, rows + h * HD : rows + (h + 1) * HD, :] for h in range(chunks)]
        return jnp.concatenate([jnp.concatenate(parts, axis=1), jnp.ones((SUB, rows), BF16)], axis=0)

    def folded(v, op):
        return op(v.reshape(rows // 8, 8, rows), axis=0)

    def usable(pair):
        key_at = lax.broadcasted_iota(jnp.int32, (rows, rows), 0)
        ok = [key_at >= count_ref[2 * pair + i] for i in range(2)]
        if first:
            tok_at = lax.broadcasted_iota(jnp.int32, (rows, rows), 1)
            ok[0] = (key_at <= tok_at) & (key_at.astype(F32) >= lst_ref[...])
            ok[1] = ok[1] & lead
        return ok

    def scores(pair, i, q):
        return lax.dot_general(
            blocks[2 * pair + i][0, 0:rows, :], q, NT, preferred_element_type=F32
        )

    def pair_values(pair, count=2):
        return jnp.concatenate([values(2 * pair + i) for i in range(count)], axis=1)

    def visit(chosen, masked, fresh, count=2):
        units = [(g, pair) for g in range(group) for pair in chosen]
        vts = {pair: pair_values(pair, count) for pair in chosen}
        best = {}
        waiting = []
        late = 4 // count
        for n in range(len(units) + late):
            if n < len(units):
                g, pair = units[n]
                probs = []
                for i in range(count):
                    s = scores(pair, i, q_all[0, g])
                    if masked:
                        s = s + bias_ref[2 * pair + i]
                    m = folded(s, jnp.max)
                    best[g] = jnp.maximum(best[g], m) if g in best else m
                    probs.append(jnp.exp2(s * c2).astype(BF16))
                if pair == chosen[-1]:
                    peak = jnp.max(best.pop(g), axis=0, keepdims=True)
                    if not first:
                        peak = jnp.where(lead, peak, FILL)
                    top_out[0, 1, g : g + 1, :] = jnp.maximum(top_out[0, 1, g : g + 1, :], peak)
                waiting.append((g, pair, jnp.concatenate(probs, axis=0)))
            if n >= late:
                g, pair, p = waiting.pop(0)
                more = jnp.dot(vts[pair], p, preferred_element_type=F32)[0:KEEP]
                if first:
                    acc_out[0, g] = more
                else:
                    old = acc_in if fresh and pair == chosen[0] else acc_out
                    acc_out[0, g] = old[0, g] + jnp.where(lead, more, 0.0)

    def revisit(pair):
        ok = usable(pair)
        if not first:
            ok = [one & lead for one in ok]
        vt = pair_values(pair)

        @pl.loop(0, group)
        def _(g):
            shift = top_out[0, 0, pl.ds(g, 1), :] * c2
            probs = [
                jnp.exp2(jnp.where(ok[i], scores(pair, i, q_all[0, g]), FILL) * c2 - shift) for i in range(2)
            ]
            p = jnp.concatenate(probs, axis=0).astype(BF16)
            acc_out[0, g] = acc_out[0, g] + jnp.dot(vt, p, preferred_element_type=F32)[0:KEEP]

    @pl.when(opening)
    def _():
        for pair in range(pairs):
            for i, ok in enumerate(usable(pair)):
                bias_ref[2 * pair + i] = jnp.where(ok, 0.0, FILL)

    if first:

        ones = jnp.ones((SUB, HD), BF16)

        def diagonal(g, i):
            prod = q_all[0, g].astype(F32) * own_ref[i, 0].astype(F32)
            high = prod.astype(BF16)
            low = (prod - high.astype(F32)).astype(BF16)
            both = jnp.concatenate([high, low], axis=1)
            wide = jnp.concatenate([ones, ones], axis=1)
            return lax.dot_general(wide, both, NT, preferred_element_type=F32)[0:1]

        for i in range(1, steps):

            @pl.when(step >= i)
            def _():
                for g in range(group):
                    own_s[i, g : g + 1, :] = diagonal(g, i)

            @pl.when(step < i)
            def _():
                own_s[i] = jnp.full((group, rows), FILL, F32)

        top_out[0, 0] = jnp.zeros((group, rows), F32)
        top_out[0, 1] = functools.reduce(jnp.maximum, [own_s[i] for i in range(1, steps)])

        def add_drafts():
            weights = [jnp.exp2((own_s[i] - top_out[0, 0]) * c2) for i in range(1, steps)]
            for g in range(group):
                acc_out[0, g, HD:KEEP] = acc_out[0, g, HD:KEEP] + functools.reduce(jnp.add, weights)[g : g + 1, :]
            for i in range(1, steps):

                @pl.when(step >= i)
                def _():
                    own_val = own_ref[i, 1].astype(F32).T
                    for g in range(group):
                        w = weights[i - 1][g : g + 1, :].astype(BF16).astype(F32)
                        acc_out[0, g, 0:HD] = acc_out[0, g, 0:HD] + own_val * w

        @pl.when(count_ref[1] < rows)
        def _():
            visit([0], True, True)

        @pl.when(count_ref[1] >= rows)
        def _():
            visit([0], True, True, 1)

        add_drafts()
        spread = jnp.max(jnp.abs(top_out[0, 1])) * c2

        @pl.when(spread > LIMIT)
        def _():
            top_out[0, 0] = top_out[0, 1]
            acc_out[...] = jnp.zeros_like(acc_out)
            revisit(0)
            add_drafts()

    else:
        top_out[...] = top_in[...]
        some, full = [], []
        for pair in range(pairs):
            a, b = count_ref[2 * pair], count_ref[2 * pair + 1]
            some.append(jnp.minimum(a, b) < rows)
            full.append(jnp.maximum(a, b) == 0)
        half = [count_ref[2 * pair + 1] >= rows for pair in range(pairs)]

        together = {}
        for begin in range(pairs % 2, pairs, 2):
            a, b = begin, begin + 1
            plain = begin < 2
            trio = jnp.logical_and(pairs == 3, full[0] & full[1] & full[pairs - 1])
            if plain:
                both = full[a] & full[b] & jnp.logical_not(trio)
            else:
                both = some[a] & some[b] & jnp.logical_not(half[a] | half[b])
            together[a] = together[b] = both
            opens = begin < 2

            @pl.when(both)
            def _():
                visit([a, b], not plain, opens)

            if pairs == 3:

                @pl.when(trio)
                def _():
                    visit([0, 1, 2], False, True)

                together = {pair: both | trio if pair else trio for pair in range(3)}

            if opens:

                @pl.when(jnp.logical_not(both | trio))
                def _():
                    for g in range(group):
                        acc_out[0, g] = acc_in[0, g]

        for pair in range(pairs):
            alone = some[pair] & jnp.logical_not(together.get(pair, False))

            @pl.when(alone & jnp.logical_not(half[pair]))
            def _():
                visit([pair], True, False)

            @pl.when(alone & half[pair])
            def _():
                visit([pair], True, False, 1)

        past = top_in[0, 0]
        spread = jnp.max(jnp.maximum(top_out[0, 1] * c2 - LIMIT, jnp.abs(past)))

        @pl.when(spread > 0.0)
        def _():
            top_out[0, 0] = top_out[0, 1]
            fade = jnp.exp2((past - top_out[0, 1]) * c2)
            for g in range(group):
                acc_out[0, g] = acc_in[0, g] * fade[g : g + 1, :]
            for pair in range(pairs):

                @pl.when(some[pair])
                def _():
                    revisit(pair)

    if last:
        for g in range(group):
            o = acc_out[0, g, 0:HD] * (1.0 / acc_out[0, g, HD : HD + 1])
            out_ref[0, :, g * HD : (g + 1) * HD] = o.astype(BF16).T
        peak_ref[0] = top_out[0, 1] * scale


def stage(queries, draft_kv, doc_ids, blocks, lstart, sources, state, losses=(), heads=None):
    steps, rows, width = queries.shape
    kvl = draft_kv.shape[3] // HD
    group = width // HD // kvl
    depth = blocks[0].shape[1]
    first = heads is not None
    low, high = heads if first else (0, kvl)
    chained = first and state is not None
    last = len(losses) > 0
    acc_shape = (kvl * steps, group, KEEP, rows)
    top_shape = (kvl * steps, 2, group, rows)
    acc_spec = pl.BlockSpec((1, group, KEEP, rows), lambda k, j, s: ((k + low) * steps + j, 0, 0, 0))
    top_spec = pl.BlockSpec((1, 2, group, rows), lambda k, j, s: ((k + low) * steps + j, 0, 0, 0))
    row_spec = pl.BlockSpec((1, rows), lambda k, j, s: (0, 0))
    wide_spec = pl.BlockSpec((1, rows, group * HD), lambda k, j, s: (j, 0, k + low))
    tile_spec = pl.BlockSpec((1, group, rows, HD), lambda k, j, s: ((k + low) * steps + j, 0, 0, 0))
    in_specs = (
        [wide_spec if first else tile_spec]
        + [pl.BlockSpec((1, depth, HD), lambda k, j, s: (k + low, 0, 0))] * len(blocks)
        + [row_spec]
    )
    args = [queries if first else state[2]] + blocks + [lstart]
    scratch = [
        pltpu.VMEM((len(blocks), rows, rows), F32),
        pltpu.SMEM((len(blocks),), jnp.int32),
    ]
    aliases = {}
    out_shape = [jax.ShapeDtypeStruct(acc_shape, F32), jax.ShapeDtypeStruct(top_shape, F32)]
    out_specs = [acc_spec, top_spec]
    if first:
        out_shape += [jax.ShapeDtypeStruct((kvl * steps, group, rows, HD), BF16)]
        out_specs += [tile_spec]
        args += [draft_kv]
        in_specs += [pl.BlockSpec((steps, 2, rows, HD), lambda k, j, s: (0, 0, 0, k + low))]
        scratch = [
            pltpu.VMEM((steps, group, rows), F32),
        ] + scratch
    if state is not None:
        aliases = {len(args) + 1: 0, len(args) + 2: 1}
        if first:
            aliases[len(args) + 3] = 2
        args += state[: 3 if first else 2]
        in_specs += [pl.BlockSpec(memory_space=pl.ANY)] * 3 if first else [acc_spec, top_spec]
    if last:
        aliases = {}
        args += losses
        in_specs += [pl.BlockSpec(losses[0].shape, lambda k, j, s: (0, 0, 0))] * len(losses)
        out_shape = [
            jax.ShapeDtypeStruct(queries.shape, BF16),
            jax.ShapeDtypeStruct((steps, kvl * group, rows), F32),
            jax.ShapeDtypeStruct((1, rows), F32),
        ]
        out_specs = [
            pl.BlockSpec((1, rows, group * HD), lambda k, j, s: (j, 0, k)),
            pl.BlockSpec((1, group, rows), lambda k, j, s: (j, k, 0)),
            row_spec,
        ]
        scratch = [
            pltpu.VMEM((1, group, KEEP, rows), F32),
            pltpu.VMEM((1, 2, group, rows), F32),
        ] + scratch
    work = (high - low) * steps * group * rows * rows * len(blocks)
    return pl.pallas_call(
        functools.partial(
            stage_kernel, group, rows, steps, sources, first, chained, len(losses)
        ),
        out_shape=out_shape,
        grid_spec=pltpu.PrefetchScalarGridSpec(
            num_scalar_prefetch=1,
            grid=(high - low, steps),
            in_specs=in_specs,
            out_specs=out_specs,
            scratch_shapes=scratch,
        ),
        input_output_aliases=aliases,
        name="stage_first" if first else ("stage_last" if last else "stage_mid"),
        compiler_params=pltpu.CompilerParams(vmem_limit_bytes=VMEM),
        cost_estimate=pl.CostEstimate(
            flops=4 * work * HD, transcendentals=work, bytes_accessed=4 * kvl * steps * group * HD * rows
        ),
    )(doc_ids, *args)


def loss_kernel(block, width, tgt_ref, x_ref, out_ref, all_ref):
    i = pl.program_id(0)
    first = i * block
    start_col = lax.axis_index("vocab") * width
    step = min(width, 2048)
    wide = min(width, 512)
    row_at = lax.broadcasted_iota(jnp.int32, (SUB, HD), 0)
    lane_at = lax.broadcasted_iota(jnp.int32, (SUB, HD), 1)

    @pl.loop(0, block // SUB)
    def _(b):
        here = pl.ds(pl.multiple_of(b * SUB, SUB), SUB)
        peak = x_ref[here, 0:step]
        total = jnp.zeros((SUB, wide), F32)
        for c in range(width // step):
            x = x_ref[here, c * step : (c + 1) * step]
            peak = jnp.maximum(peak, x)
            for h in range(step // wide):
                total = total + jnp.exp2(x[:, h * wide : (h + 1) * wide].astype(F32) * LOG2E)
        peak = jnp.max(peak.astype(F32), axis=1, keepdims=True)
        total = jnp.sum(total, axis=1, keepdims=True)
        near = jnp.zeros((SUB, HD), F32)
        spot = jnp.full((SUB, HD), -1, jnp.int32)
        for r in range(SUB):
            t = tgt_ref[first + b * SUB + r] - start_col
            inside = (t >= 0) & (t < width)
            lane = jnp.where(inside, t, 0)
            start = pl.multiple_of((lane // HD) * HD, HD)
            near = jnp.where(row_at == r, x_ref[here, pl.ds(start, HD)].astype(F32), near)
            spot = jnp.where(row_at == r, jnp.where(inside, lane - start, -1), spot)
        hit = jnp.sum(jnp.where(lane_at == spot, near, 0.0), axis=1, keepdims=True)
        there = pl.ds(pl.multiple_of(first + b * SUB, SUB), SUB)
        all_ref[there, :] = jnp.where(lane_at == 1, total, jnp.where(lane_at == 2, hit, 0.0))

        @pl.when(jnp.max(jnp.abs(peak)) * LOG2E > LIMIT)
        def _():
            exact = jnp.zeros((SUB, wide), F32)
            for c in range(width // wide):
                x = x_ref[here, c * wide : (c + 1) * wide].astype(F32)
                exact = exact + jnp.exp2((x - peak) * LOG2E)
            exact = jnp.sum(exact, axis=1, keepdims=True)
            all_ref[there, :] = jnp.where(lane_at == 0, peak, jnp.where(lane_at == 1, exact, hit))

    @pl.when(i == pl.num_programs(0) - 1)
    def _():
        out_ref[0] = all_ref[...].T[0:8]


def loss_parts(logits, targets):
    rows, width = logits.shape
    block = 64
    return pl.pallas_call(
        functools.partial(loss_kernel, block, width),
        grid_spec=pltpu.PrefetchScalarGridSpec(
            num_scalar_prefetch=1,
            grid=(rows // block,),
            in_specs=[pl.BlockSpec((block, width), lambda i, t: (i, 0))],
            out_specs=pl.BlockSpec((1, 8, rows), lambda i, t: (0, 0, 0)),
            scratch_shapes=[pltpu.VMEM((rows, HD), F32)],
        ),
        out_shape=jax.ShapeDtypeStruct((1, 8, rows), F32),
        name="loss",
        compiler_params=pltpu.CompilerParams(vmem_limit_bytes=VMEM),
        cost_estimate=pl.CostEstimate(
            flops=4 * logits.size, transcendentals=logits.size, bytes_accessed=2 * logits.size
        ),
    )(targets, logits)


def program(queries, draft_kv, doc_ids, logits, targets):
    shards = lax.axis_size("seq")
    halves = lax.axis_size("vocab")
    levels = shards // 4

    def up(x):
        return lax.ppermute(x, "seq", [(i, i + 4) for i in range(shards - 4)])

    def swap(x, bit):
        return lax.ppermute(x, "seq", [(i, i ^ bit) for i in range(shards)])

    mine, lstart = pack(draft_kv, doc_ids)
    z, x, c, d = [mine], [], [], []

    def spread(level):
        if level + 1 < levels:
            z.append(up(z[level]))
        c.append(swap(z[level], 1))
        x.append(swap(z[level], 2))
        if level > 0:
            d.append(swap(x[level - 1], 1))
        if level + 1 == levels:
            d.append(swap(z[level], 3))

    spread(0)
    parts = loss_parts(logits, targets)
    z[1], x[0], parts = lax.optimization_barrier((z[1], x[0], parts))
    spread(1)
    losses = [parts] + [
        lax.ppermute(parts, "vocab", [(i, (i + t) % halves) for i in range(halves)])
        for t in range(1, halves)
    ]

    def run(picked, state, **more):
        names = {"z": (z, 0), "c": (c, 1), "x": (x, 2), "d": (d, 3)}
        blocks = [names[name][0][level] for name, level in picked]
        sources = [(names[name][1], level) for name, level in picked]
        return stage(queries, draft_kv, doc_ids, blocks, lstart, sources, state, **more)

    kvl = draft_kv.shape[3] // HD
    cuts = [0, kvl // 2, kvl] if kvl > 1 else [0, kvl]
    state = None
    for low, high in zip(cuts, cuts[1:]):
        state = run([("z", 0), ("c", 0)], state, heads=(low, high))
        level = len(c)
        if level < levels:
            z[level], x[level - 1], top = lax.optimization_barrier((z[level], x[level - 1], state[1]))
            state = [state[0], top, state[2]]
            spread(level)
    while len(c) < levels:
        spread(len(c))
    rest = [("x", 0), ("d", 0)]
    for level in range(1, levels):
        rest += [(name, level) for name in "zcxd"]
    split = [0, 6] + list(range(14, len(rest) + 1, 8))
    for begin, end in zip(split, split[1:]):
        final = end == len(rest)
        moved = run(rest[begin:end], state, losses=losses if final else [])
        state = moved if final else [*moved, state[2]]
    out, peaks, token_loss = state
    return (out, peaks.transpose(0, 2, 1), token_loss.reshape(-1))


def solution(mesh):
    in_specs = (
        P(None, "seq", "vocab"),
        P(None, None, "seq", "vocab"),
        P("seq"),
        P("seq", "vocab"),
        P("seq"),
    )
    out_specs = (P(None, "seq", "vocab"), P(None, "seq", "vocab"), P("seq"))
    return jax.shard_map(program, mesh=mesh, in_specs=in_specs, out_specs=out_specs, check_vma=False)
```
